128 devices in a mesh: variant: 8 (over z_lo, x), vocab: 16 (over y, z_hi, core).
Axes of the slice: x: 4, y: 4, z: 4 (z_hi: 2, z_lo: 2; z = z_hi * 2 + z_lo), core: 2. Of those that a mesh axis runs over, the one named last changes fastest.
Arguments:
- teacher_hidden: bfloat16 [8, 256, 4096], P(None, None, ('variant', 'vocab')), may hold values from -24 to 24
- teacher_weight: bfloat16 [4096, 64128], P(None, ('vocab', 'variant')), may hold values from -1 to 1
- variant_ids: int32 [8], replicated, may hold values from 0 to 13
- temps: float32 [14], replicated, may hold values from 0.7 to 1.5
- student_hidden: bfloat16 [256, 2048], P(None, 'variant'), may hold values from -24 to 24
- student_weight: bfloat16 [2048, 64128], P('variant', 'vocab'), may hold values from -1 to 1
- token_ids: int32 [256], P('variant'), may hold values from 0 to 64127
- loss_mask: int32 [256], P('variant'), may hold values 0 or 1
Outputs:
- token_loss: float32 [256], P('variant')
- student_grad: float32 [2048, 64128], P('variant', 'vocab')
The draws below stay inside these ranges and needn't reach their ends.
All inputs are finite; a program needn't handle non-finite values. No bound on the sum of `loss_mask` on one device may be relied on, other than what follows from the above.
Results may differ from the reference program's by a relative error of at most 0.0025.
Values may be sent and summed in bfloat16 or wider, within the bound.
No kernel may reach another device: no remote copies, remote signals or barrier semaphores. Data moves between devices by JAX's collectives and lax.ppermute only.
A program may use at most 192 MiB of HBM per device.

```python
import math
import jax
import jax.numpy as jnp
import numpy as np
from jax import lax

DT = 4096
DS = 2048
VOCAB = 64128
POLICIES = 14
TOK = 256
VARIANTS = 8


def hidden_draw(key, shape, salt):
    base = jax.random.normal(jax.random.fold_in(key, salt), shape, jnp.float32) * 3.0
    return jnp.clip(base, -24.0, 24.0)


def weight_draw(key, width, salt):
    base = jnp.clip(jax.random.normal(jax.random.fold_in(key, salt + 3), (width, VOCAB), jnp.float32), -6.0, 6.0) * width ** (-0.5)
    return base


def draw_teacher_hidden(key, part):
    return hidden_draw(key, (VARIANTS, TOK, DT), 100).astype(jnp.bfloat16)


def draw_teacher_weight(key, part):
    return weight_draw(key, DT, 100).astype(jnp.bfloat16)


def draw_student_hidden(key, part):
    return hidden_draw(key, (TOK, DS), 200).astype(jnp.bfloat16)


def draw_student_weight(key, part):
    return weight_draw(key, DS, 200).astype(jnp.bfloat16)


def with_ends(values, rng, low, top_value):
    shape = values.shape
    index_at = [jax.random.randint(jax.random.fold_in(rng, axis), (), 0, shape[axis]) for axis in range(len(shape))]
    values = values.at[tuple(index_at)].set(low)
    longest = shape.index(max(shape))
    index_at[longest] = (index_at[longest] + 1) % shape[longest]
    return values.at[tuple(index_at)].set(top_value)


def cumulative_ranks(count, lean):
    portions = [(1 << 20) // math.isqrt(grade ** lean) + 1 for grade in range(1, count + 1)]
    scale = 1 + sum(portions) // (1 << 30)
    return np.cumsum(np.array([max(1, weight // scale) for weight in portions]))


def ranked(stream_key, extent, amount, lean):
    grid = cumulative_ranks(amount, lean)
    pick = jax.random.randint(jax.random.fold_in(stream_key, 1), extent, 0, int(grid[amount - 1]))
    rank = jnp.searchsorted(jnp.asarray(grid, jnp.int32), pick, side="right")
    return jax.random.permutation(jax.random.fold_in(stream_key, 2), amount)[rank].astype(jnp.int32)


def setup_inputs(seed: int = 0) -> dict:
    streams_of = jax.random.split(jax.random.key(seed), 9)
    teacher_hidden = draw_teacher_hidden(jax.random.fold_in(streams_of[8], 71), 0)
    teacher_weight = draw_teacher_weight(jax.random.fold_in(streams_of[8], 71), 0)
    variant_ids = with_ends(jax.random.randint(streams_of[2], (VARIANTS,), 0, POLICIES), jax.random.fold_in(streams_of[2], 1), 0, POLICIES - 1).astype(jnp.int32)
    temps = jnp.clip(jnp.exp(jax.random.uniform(streams_of[3], (POLICIES,), jnp.float32, math.log(0.7), math.log(1.5))), 0.7, 1.5)
    student_hidden = draw_student_hidden(jax.random.fold_in(streams_of[8], 71), 0)
    student_weight = draw_student_weight(jax.random.fold_in(streams_of[8], 71), 0)
    token_ids = with_ends(ranked(streams_of[6], (TOK,), VOCAB, 2), jax.random.fold_in(streams_of[6], 3), 0, VOCAB - 1).astype(jnp.int32)
    loss_mask = with_ends((jax.random.randint(streams_of[7], (TOK,), 0, 4) < 3).astype(jnp.int32), jax.random.fold_in(streams_of[7], 1), 0, 1)
    return dict(teacher_hidden=teacher_hidden, teacher_weight=teacher_weight, variant_ids=variant_ids, temps=temps, student_hidden=student_hidden, student_weight=student_weight, token_ids=token_ids, loss_mask=loss_mask)


mix_weight = 0.5
loss_scale = 4096.0


def reference(teacher_hidden, teacher_weight, variant_ids, temps, student_hidden, student_weight, token_ids, loss_mask):
    chosen = temps[variant_ids]

    def add_variant(carry, inputs):
        hidden, tau = inputs
        scaled = jnp.dot(hidden, teacher_weight, preferred_element_type=jnp.float32) / tau
        top = jnp.max(scaled, axis=1, keepdims=True)
        expd = jnp.exp(scaled - top)
        return carry + expd / jnp.sum(expd, axis=1, keepdims=True), None

    start = jnp.zeros((teacher_hidden.shape[1], teacher_weight.shape[1]), jnp.float32)
    summed, _ = lax.scan(add_variant, start, (teacher_hidden, chosen))
    averaged = summed / VARIANTS
    logits = jnp.dot(student_hidden, student_weight, preferred_element_type=jnp.float32)
    top = jnp.max(logits, axis=1, keepdims=True)
    total = jnp.sum(jnp.exp(logits - top), axis=1, keepdims=True)
    log_probs = logits - (top + jnp.log(total))
    probs = jnp.exp(log_probs)
    onehot = token_ids[:, None] == jnp.arange(VOCAB, dtype=jnp.int32)[None, :]
    soft = jnp.sum(averaged * log_probs, axis=1)
    hard = jnp.sum(jnp.where(onehot, log_probs, 0.0), axis=1)
    maskf = loss_mask.astype(jnp.float32)
    token_loss = maskf * (-mix_weight * soft - (1.0 - mix_weight) * hard)
    error = (loss_scale * maskf[:, None] * (probs - mix_weight * averaged - (1.0 - mix_weight) * onehot.astype(jnp.float32))).astype(jnp.bfloat16)
    student_grad = jnp.dot(student_hidden.T, error, preferred_element_type=jnp.float32)
    return token_loss, student_grad
```

```python
import functools
import jax
import jax.numpy as jnp
from jax import lax
from jax.experimental import pallas as pl
from jax.experimental.pallas import tpu as pltpu
from jax.sharding import PartitionSpec as P

mix_weight = 0.5
loss_scale = 4096.0

AXES = ("variant", "vocab")
SIDE = 4
SPLIT = 768
OFFSETS = (0, -1, 1, 2)


def device_index(x, y, z, c):
    x, y, z = x % SIDE, y % SIDE, z % SIDE
    return ((z % 2) * SIDE + x) * 16 + y * 4 + (z // 2) * 2 + c


def permutation(move):
    return [
        (device_index(x, y, z, c), device_index(*move(x, y, z, c)))
        for x in range(SIDE)
        for y in range(SIDE)
        for z in range(SIDE)
        for c in range(2)
    ]


def ring_shift(axes, step):
    def move(x, y, z, c):
        at = {"x": x, "y": y, "z": z}
        at[axes[c]] += step
        return at["x"], at["y"], at["z"], c

    return permutation(move)


def sibling(value):
    return lax.ppermute(value, AXES, permutation(lambda x, y, z, c: (x, y, z, 1 - c)))


def ring_gather(value, axes):
    return [value] + [
        lax.ppermute(value, AXES, ring_shift(axes, step)) for step in (1, -1, 2)
    ]


def ordered(core, own, other, axis):
    return jnp.where(
        core == 0,
        jnp.concatenate([own, other], axis=axis),
        jnp.concatenate([other, own], axis=axis),
    )


def teacher_kernel(table, inv_tau, *refs):
    first, second = refs[0:4], refs[4:8]
    w_refs, l_refs = refs[8:10], refs[10:12]
    e_refs, stat_ref = refs[12:14], refs[14]
    hidden, w_own, w_sib, sem = refs[15:19]
    w_bufs = (w_own, w_sib)
    copies = [pltpu.make_async_copy(w_refs[i], w_bufs[i], sem.at[i]) for i in range(2)]
    for copy in copies:
        copy.start()

    def chunk_copy(part, ref, s3, n, lanes):
        row = pl.multiple_of(table[part, s3 * 16 + n] * 64, 64)
        return pltpu.make_async_copy(
            ref.at[n], hidden.at[pl.ds(row, 64), lanes], sem.at[2 + part]
        )

    parts = ((first, pl.ds(0, SPLIT)), (second, pl.ds(SPLIT, 1024 - SPLIT)))
    for part, (group, lanes) in enumerate(parts):
        for s3 in range(4):
            def start(n, _, part=part, ref=group[s3], s3=s3, lanes=lanes):
                chunk_copy(part, ref, s3, n, lanes).start()
                return 0
            lax.fori_loop(0, 16, start, 0)
    for part, (group, lanes) in enumerate(parts):
        for s3 in range(4):
            def wait(n, _, part=part, ref=group[s3], s3=s3, lanes=lanes):
                chunk_copy(part, ref, s3, n, lanes).wait()
                return 0
            lax.fori_loop(0, 16, wait, 0)
    for copy in copies:
        copy.wait()

    def tile(j, _):
        lanes = pl.ds(pl.multiple_of(j * 256, 256), 256)
        scale = inv_tau[:, lanes]
        block = hidden[:, lanes]
        scores = [
            jnp.dot(w[...], block, preferred_element_type=jnp.float32) * scale for w in w_bufs
        ]
        top = jnp.maximum(
            jnp.max(scores[0], axis=0, keepdims=True), jnp.max(scores[1], axis=0, keepdims=True)
        )
        total = jnp.zeros((1, 256), jnp.float32)
        cross = jnp.zeros((1, 256), jnp.float32)
        for i in range(2):
            e = jnp.exp(scores[i] - top)
            e_refs[i][:, lanes] = e
            logits = l_refs[i][...]
            total += jnp.sum(e, axis=0, keepdims=True)
            cross += jnp.sum(
                e * jnp.concatenate([logits, logits], axis=1), axis=0, keepdims=True
            )
        stat_ref[0:1, lanes] = top
        stat_ref[1:2, lanes] = total
        stat_ref[2:3, lanes] = cross
        return 0

    lax.fori_loop(0, 4, tile, 0)


def teacher_scores(table, inv_tau, first, second, weights, logits):
    cols, width = weights[0].shape
    vmem = pl.BlockSpec(memory_space=pltpu.VMEM)
    hbm = pl.BlockSpec(memory_space=pl.ANY)
    return pl.pallas_call(
        teacher_kernel,
        out_shape=[
            jax.ShapeDtypeStruct((cols, 1024), jnp.float32),
            jax.ShapeDtypeStruct((cols, 1024), jnp.float32),
            jax.ShapeDtypeStruct((8, 1024), jnp.float32),
        ],
        in_specs=[pl.BlockSpec(memory_space=pltpu.SMEM), vmem] + [hbm] * 10 + [vmem] * 2,
        out_specs=[vmem] * 3,
        scratch_shapes=[
            pltpu.VMEM((width, 1024), jnp.bfloat16),
            pltpu.VMEM((cols, width), jnp.bfloat16),
            pltpu.VMEM((cols, width), jnp.bfloat16),
            pltpu.SemaphoreType.DMA((4,)),
        ],
        compiler_params=pltpu.CompilerParams(vmem_limit_bytes=44 << 20),
        cost_estimate=pl.CostEstimate(
            flops=2 * 2 * cols * width * 1024,
            bytes_accessed=2 * (2 * cols * width + width * 1024) + 8 * cols * 1024,
            transcendentals=2 * cols * 1024,
        ),
    )(table, inv_tau, *first, *second, *weights, *logits)


def on_device(
    teacher_hidden,
    teacher_weight,
    variant_ids,
    temps,
    student_hidden,
    student_weight,
    token_ids,
    loss_mask,
):
    a = lax.axis_index("variant")
    b = lax.axis_index("vocab")
    core = b % 2
    x, y, z = a % 4, b // 4, (b // 2) % 2 * 2 + a // 4
    cols = teacher_weight.shape[1]
    half = 128

    meta = jnp.concatenate(
        [token_ids // 256, token_ids % 256, loss_mask, jnp.zeros((160,), jnp.int32)]
    ).astype(jnp.bfloat16)[None, None]
    mine = lax.dynamic_slice_in_dim(student_hidden, core * half, half, axis=0)
    send = jnp.concatenate(
        [
            jnp.broadcast_to(mine[None], (8, half, 256)),
            student_weight.T.reshape(8, cols, 256),
            jnp.broadcast_to(meta, (8, 1, 256)),
        ],
        axis=1,
    )
    got = lax.all_to_all(send, "variant", 0, 0, tiled=True)
    flat = jnp.transpose(got, (1, 0, 2)).reshape(half + cols + 1, 2048)
    hs, ws = flat[:half], flat[half : half + cols]
    ws_other = sibling(ws)
    meta_all = got[:, half + cols]
    ids = (meta_all[:, 0:32].astype(jnp.int32) * 256 + meta_all[:, 32:64].astype(jnp.int32)).reshape(256)
    maskf = meta_all[:, 64:96].astype(jnp.float32).reshape(256)
    ids_half = lax.dynamic_slice_in_dim(ids, core * half, half)
    mask_half = lax.dynamic_slice_in_dim(maskf, core * half, half)

    halves = [
        lax.dynamic_slice_in_dim(teacher_hidden, start * half, half, axis=1)
        .transpose(2, 0, 1)
        .reshape(32, 1024)
        for start in (core, 1 - core)
    ]
    unit = ordered(core, halves[0], sibling(halves[1]), 0)
    w_own = teacher_weight.T
    w_other = sibling(w_own)
    stage1 = jnp.stack(ring_gather(unit, "zx"))
    first = jnp.stack(ring_gather(stage1[:, :, :SPLIT], "yy")).reshape(16, 64, SPLIT)
    second = jnp.stack(ring_gather(stage1[:, :, SPLIT:], "xz")).reshape(16, 64, 1024 - SPLIT)
    first = ring_gather(first, "xz")
    second = ring_gather(second, "yy")

    offsets = jnp.array(OFFSETS, jnp.int32)
    o1, o2, o3 = (
        offsets.reshape(shape) for shape in ((1, 1, 4), (1, 4, 1), (4, 1, 1))
    )
    zero = jnp.zeros((4, 4, 4), jnp.int32)

    def place(dx, dy, dz):
        px, py, pz = (x + dx) % 4, (y + dy) % 4, (z + dz) % 4
        return ((pz % 2 * 4 + px) * 8 + py * 2 + pz // 2 + zero).reshape(64)

    table = jnp.where(
        core == 0,
        jnp.stack([place(o3, o2, o1), place(o2, o3, o1)]),
        jnp.stack([place(o1, o2, o3), place(o1, o3, o2)]),
    )
    categories = jnp.arange(temps.shape[0], dtype=jnp.int32)
    taus = jnp.sum(
        jnp.where(variant_ids[:, None] == categories[None, :], temps[None, :], 0.0), axis=1
    )
    inv_tau = jnp.repeat(1.0 / taus, half)[None]

    dims = (((1,), (1,)), ((), ()))
    logits = [
        lax.dot_general(w, hs, dims, preferred_element_type=jnp.float32) for w in (ws, ws_other)
    ]
    s_top = jnp.maximum(jnp.max(logits[0], axis=0), jnp.max(logits[1], axis=0))
    s_sum = sum(jnp.sum(jnp.exp(l - s_top), axis=0) for l in logits)
    rows = jnp.arange(cols, dtype=jnp.int32)[:, None]
    onehots = [
        (block * 8 + a) * cols + rows == ids_half[None, :] for block in (b, b + 1 - 2 * core)
    ]
    s_hard = sum(jnp.sum(jnp.where(o, l, 0.0), axis=0) for o, l in zip(onehots, logits))

    e_own, e_other, stats = teacher_scores(
        table, inv_tau, first, second, (w_own, w_other), logits
    )
    e = (e_own, e_other)
    t_stats = stats[:3].reshape(24, half)
    packed = jnp.concatenate(
        [t_stats, jnp.stack([s_top, s_sum, s_hard]), jnp.zeros((5, half), jnp.float32)]
    )
    def merge(g):
        n = g.shape[0]
        top = jnp.max(g[:, 0:8], axis=0)
        scale = jnp.exp(g[:, 0:8] - top)
        total = jnp.sum(g[:, 8:16] * scale, axis=0)
        cross = jnp.sum(g[:, 16:24] * scale, axis=0)
        stop = jnp.max(g[:, 24], axis=0)
        ssum = jnp.sum(g[:, 25] * jnp.exp(g[:, 24] - stop), axis=0)
        hard = jnp.sum(g[:, 26], axis=0)
        return jnp.concatenate(
            [top, total, cross, jnp.stack([stop, ssum, hard]), jnp.zeros((5, half), jnp.float32)]
        )

    tile8 = jnp.broadcast_to(packed[None], (8, 32, half))
    by_variant = merge(lax.all_to_all(tile8, "variant", 0, 0, tiled=True))
    tile16 = jnp.broadcast_to(by_variant[None], (16, 32, half))
    over = lax.all_to_all(tile16, "vocab", 0, 0, tiled=True).reshape(8, 2, 32, half)
    merged = merge(lax.dynamic_index_in_dim(over, core, 1, keepdims=False))
    top, total, cross = merged[0:8], merged[8:16], merged[16:24]
    lse = merged[24] + jnp.log(merged[25])
    hard = merged[26] - lse
    soft = jnp.sum(cross / total, axis=0) / 8 - lse
    loss_half = mask_half * (-mix_weight * soft - (1.0 - mix_weight) * hard)
    loss_all = ordered(core, loss_half, sibling(loss_half), 0)
    token_loss = lax.dynamic_slice_in_dim(loss_all, a * 32, 32)

    local_top = stats[0].reshape(8, half)
    coef = jnp.exp(local_top - top) / (8 * total)
    errors = []
    for i in range(2):
        averaged = sum(e[i][:, v * half : (v + 1) * half] * coef[v] for v in range(8))
        q = jnp.exp(logits[i] - lse)
        errors.append(
            (
                loss_scale
                * mask_half
                * (q - mix_weight * averaged - (1.0 - mix_weight) * onehots[i].astype(jnp.float32))
            ).astype(jnp.bfloat16)
        )
    error = ordered(core, errors[0], sibling(errors[1]), 1)
    error_all = lax.all_to_all(
        jnp.broadcast_to(error[None], (8, cols, 256)), "variant", 0, 0, tiled=True
    ).reshape(8 * cols, 256)
    grad_t = jnp.dot(error_all, student_hidden, preferred_element_type=jnp.float32)
    return token_loss, grad_t.T


def solution(mesh):
    in_specs = (
        P(None, None, ("variant", "vocab")),
        P(None, ("vocab", "variant")),
        P(),
        P(),
        P(None, "variant"),
        P("variant", "vocab"),
        P("variant"),
        P("variant"),
    )
    out_specs = (P("variant"), P("variant", "vocab"))
    return jax.shard_map(
        on_device, mesh=mesh, in_specs=in_specs, out_specs=out_specs, check_vma=False
    )
```

```python
import math
import jax
import jax.numpy as jnp
from jax import lax
from jax.experimental import pallas as pl
from jax.experimental.pallas import tpu as pltpu
from jax.sharding import PartitionSpec as P

mix_weight = 0.5
loss_scale = 4096.0

AXES = ("variant", "vocab")
SIDE = 4
SPLIT = 768
ROWS = 640
OFFSETS = (0, -1, 1, 2)


def device_index(x, y, z, c):
    x, y, z = x % SIDE, y % SIDE, z % SIDE
    return ((z % 2) * SIDE + x) * 16 + y * 4 + (z // 2) * 2 + c


def permutation(move):
    return [
        (device_index(x, y, z, c), device_index(*move(x, y, z, c)))
        for x in range(SIDE)
        for y in range(SIDE)
        for z in range(SIDE)
        for c in range(2)
    ]


def ring_shift(axes, step):
    def move(x, y, z, c):
        at = {"x": x, "y": y, "z": z}
        at[axes[c]] += step
        return at["x"], at["y"], at["z"], c

    return permutation(move)


def sibling(value):
    return lax.ppermute(value, AXES, permutation(lambda x, y, z, c: (x, y, z, 1 - c)))


def ring_gather(value, axes):
    return [value] + [
        lax.ppermute(value, AXES, ring_shift(axes, step)) for step in (1, -1, 2)
    ]


def pack_kernel(*refs):
    blocks, first_ref, second_ref = refs[0:4], refs[5], refs[6]
    for i, block in enumerate(blocks):
        first_ref[i] = block[:, :SPLIT]
        second_ref[i] = block[:, SPLIT:]


def pack(blocks, after):
    vmem = pl.BlockSpec(memory_space=pltpu.VMEM)
    rows, lanes = blocks[0].shape
    return pl.pallas_call(
        pack_kernel,
        out_shape=[
            jax.ShapeDtypeStruct((4, rows, SPLIT), jnp.bfloat16),
            jax.ShapeDtypeStruct((4, rows, lanes - SPLIT), jnp.bfloat16),
        ],
        in_specs=[vmem] * 4 + [pl.BlockSpec(memory_space=pl.ANY)],
        out_specs=[vmem] * 2,
        cost_estimate=pl.CostEstimate(
            flops=0, bytes_accessed=16 * rows * lanes, transcendentals=0
        ),
    )(*blocks, after)


def stack_kernel(*refs):
    for part in range(2):
        for i in range(4):
            refs[8 + part][i] = refs[4 * part + i][...]


def stack_parts(first, second):
    vmem = pl.BlockSpec(memory_space=pltpu.VMEM)
    shapes = [(4,) + group[0].shape for group in (first, second)]
    return pl.pallas_call(
        stack_kernel,
        out_shape=[jax.ShapeDtypeStruct(shape, jnp.bfloat16) for shape in shapes],
        in_specs=[vmem] * 8,
        out_specs=[vmem] * 2,
        cost_estimate=pl.CostEstimate(
            flops=0, bytes_accessed=4 * sum(math.prod(shape) for shape in shapes), transcendentals=0
        ),
    )(*first, *second)


def halves_kernel(before, after, *refs):
    before_half, after_half = refs[-4:-2]
    before_half[...] = before[...]
    after_half[...] = after[...]


def forward_halves(before, after, through, others):
    n, rows, lanes = before.shape
    block = (n // 2, rows, lanes)
    hbm = pl.BlockSpec(memory_space=pl.ANY)
    lower = pl.BlockSpec(block, lambda i: (0, 0, 0))
    return pl.pallas_call(
        halves_kernel,
        grid=(1,),
        out_shape=[jax.ShapeDtypeStruct(block, before.dtype)] * 2
        + [jax.ShapeDtypeStruct(t.shape, t.dtype) for t in through],
        in_specs=[lower, pl.BlockSpec(block, lambda i: (1, 0, 0))] + [hbm] * (2 + len(others)),
        out_specs=[lower, lower, hbm, hbm],
        input_output_aliases={2: 2, 3: 3},
        cost_estimate=pl.CostEstimate(
            flops=0, bytes_accessed=4 * n * rows * lanes, transcendentals=0
        ),
    )(before, after, *through, *others)


def student_kernel(own_ref, other_ref, ids_ref, base_ref, l_own, l_other, stat_ref):
    half, cols = l_own.shape[1], l_own.shape[0]
    dims = (((1,), (1,)), ((), ()))
    logits = []
    for ref, out in ((own_ref, l_own), (other_ref, l_other)):
        total = jnp.zeros((cols, half), jnp.float32)
        for block in range(8):
            total += lax.dot_general(
                ref[block, half : half + cols, :],
                own_ref[block, :half, :],
                dims,
                preferred_element_type=jnp.float32,
            )
        out[...] = total
        logits.append(total)
    top = jnp.maximum(
        jnp.max(logits[0], axis=0, keepdims=True), jnp.max(logits[1], axis=0, keepdims=True)
    )
    total = jnp.zeros((1, half), jnp.float32)
    hard = jnp.zeros((1, half), jnp.float32)
    rows = lax.broadcasted_iota(jnp.int32, (cols, half), 0)
    for i in range(2):
        total += jnp.sum(jnp.exp(logits[i] - top), axis=0, keepdims=True)
        hit = rows + base_ref[i] == ids_ref[...]
        hard += jnp.sum(jnp.where(hit, logits[i], 0.0), axis=0, keepdims=True)
    stat_ref[...] = jnp.concatenate([top, total, hard, jnp.zeros((5, half), jnp.float32)])


def student_logits(own, other, ids, base, cols):
    half = ids.shape[1]
    vmem = pl.BlockSpec(memory_space=pltpu.VMEM)
    return pl.pallas_call(
        student_kernel,
        out_shape=[
            jax.ShapeDtypeStruct((cols, half), jnp.float32),
            jax.ShapeDtypeStruct((cols, half), jnp.float32),
            jax.ShapeDtypeStruct((8, half), jnp.float32),
        ],
        in_specs=[vmem] * 3 + [pl.BlockSpec(memory_space=pltpu.SMEM)],
        out_specs=[vmem] * 3,
        compiler_params=pltpu.CompilerParams(vmem_limit_bytes=24 << 20),
        cost_estimate=pl.CostEstimate(
            flops=2 * 2 * cols * half * 2048, bytes_accessed=12 << 20, transcendentals=2 * cols * half
        ),
    )(own, other, ids, base)


def ordered(core, own, other, axis):
    return jnp.where(
        core == 0,
        jnp.concatenate([own, other], axis=axis),
        jnp.concatenate([other, own], axis=axis),
    )


def teacher_kernel(table, inv_tau, *refs):
    first, second = refs[0:5], refs[5:9]
    w_refs, l_refs = refs[9:11], refs[11:13]
    e_refs, stat_ref = refs[13:15], refs[15]
    hidden, w_own, w_sib, sem = refs[16:20]
    w_bufs = (w_own, w_sib)
    copies = [pltpu.make_async_copy(w_refs[i], w_bufs[i], sem.at[i]) for i in range(2)]
    for copy in copies:
        copy.start()

    def chunk_copy(part, ref, base, n, lanes):
        row = pl.multiple_of(table[part, base + n] * 64, 64)
        return pltpu.make_async_copy(
            ref.at[n], hidden.at[pl.ds(row, 64), lanes], sem.at[2 + part]
        )

    parts = ((first, pl.ds(0, SPLIT)), (second, pl.ds(SPLIT, 1024 - SPLIT)))
    blocks = []
    for part, (group, lanes) in enumerate(parts):
        base = 0
        for ref in group:
            blocks.append((part, ref, base, lanes))
            base += ref.shape[0]
    for part, ref, base, lanes in blocks:
        def start(n, _, part=part, ref=ref, base=base, lanes=lanes):
            chunk_copy(part, ref, base, n, lanes).start()
            return 0
        lax.fori_loop(0, ref.shape[0], start, 0)
    for part, ref, base, lanes in blocks:
        def wait(n, _, part=part, ref=ref, base=base, lanes=lanes):
            chunk_copy(part, ref, base, n, lanes).wait()
            return 0
        lax.fori_loop(0, ref.shape[0], wait, 0)
    for copy in copies:
        copy.wait()

    def tile(j, _):
        lanes = pl.ds(pl.multiple_of(j * 256, 256), 256)
        scale = inv_tau[:, lanes]
        block = hidden[:, lanes]
        scores = [
            jnp.dot(w[...], block, preferred_element_type=jnp.float32) * scale for w in w_bufs
        ]
        top = jnp.maximum(
            jnp.max(scores[0], axis=0, keepdims=True), jnp.max(scores[1], axis=0, keepdims=True)
        )
        total = jnp.zeros((1, 256), jnp.float32)
        cross = jnp.zeros((1, 256), jnp.float32)
        for i in range(2):
            e = jnp.exp(scores[i] - top)
            e_refs[i][:, lanes] = e
            logits = l_refs[i][...]
            total += jnp.sum(e, axis=0, keepdims=True)
            cross += jnp.sum(
                e * jnp.concatenate([logits, logits], axis=1), axis=0, keepdims=True
            )
        stat_ref[0:1, lanes] = top
        stat_ref[1:2, lanes] = total
        stat_ref[2:3, lanes] = cross
        return 0

    lax.fori_loop(0, 4, tile, 0)


def teacher_scores(table, inv_tau, first, second, weights, logits):
    cols, width = weights[0].shape
    vmem = pl.BlockSpec(memory_space=pltpu.VMEM)
    hbm = pl.BlockSpec(memory_space=pl.ANY)
    return pl.pallas_call(
        teacher_kernel,
        out_shape=[
            jax.ShapeDtypeStruct((cols, 1024), jnp.float32),
            jax.ShapeDtypeStruct((cols, 1024), jnp.float32),
            jax.ShapeDtypeStruct((8, 1024), jnp.float32),
        ],
        in_specs=[pl.BlockSpec(memory_space=pltpu.SMEM), vmem] + [hbm] * 11 + [vmem] * 2,
        out_specs=[vmem] * 3,
        scratch_shapes=[
            pltpu.VMEM((width, 1024), jnp.bfloat16),
            pltpu.VMEM((cols, width), jnp.bfloat16),
            pltpu.VMEM((cols, width), jnp.bfloat16),
            pltpu.SemaphoreType.DMA((4,)),
        ],
        compiler_params=pltpu.CompilerParams(vmem_limit_bytes=44 << 20),
        cost_estimate=pl.CostEstimate(
            flops=2 * 2 * cols * width * 1024,
            bytes_accessed=2 * (2 * cols * width + width * 1024) + 8 * cols * 1024,
            transcendentals=2 * cols * 1024,
        ),
    )(table, inv_tau, *first, *second, *weights, *logits)


def on_device(
    teacher_hidden,
    teacher_weight,
    variant_ids,
    temps,
    student_hidden,
    student_weight,
    token_ids,
    loss_mask,
):
    a = lax.axis_index("variant")
    b = lax.axis_index("vocab")
    core = b % 2
    x, y, z = a % 4, b // 4, (b // 2) % 2 * 2 + a // 4
    cols = teacher_weight.shape[1]
    half = 128

    halves = [
        lax.dynamic_slice_in_dim(teacher_hidden, start * half, half, axis=1)
        .transpose(2, 0, 1)
        .reshape(32, 1024)
        for start in (core, 1 - core)
    ]
    unit = ordered(core, halves[0], sibling(halves[1]), 0)
    w_own = teacher_weight.T
    w_other = sibling(w_own)
    first, second = pack(ring_gather(unit, "zx"), w_other)

    meta = jnp.concatenate(
        [token_ids // 256, token_ids % 256, loss_mask, jnp.zeros((32,), jnp.int32)]
    ).astype(jnp.bfloat16)
    meta = jnp.concatenate([meta, first[0, 0, :128]])[None, None]
    mine = lax.dynamic_slice_in_dim(student_hidden, core * half, half, axis=0)
    send = jnp.concatenate(
        [
            jnp.broadcast_to(mine[None], (8, half, 256)),
            student_weight.T.reshape(8, cols, 256),
            jnp.broadcast_to(meta, (8, ROWS - half - cols, 256)),
        ],
        axis=1,
    )
    got = lax.all_to_all(send, "variant", 0, 0, tiled=True)

    first, second = stack_parts(ring_gather(first, "yy"), ring_gather(second, "xz"))
    first = first.reshape(16, 64, SPLIT)
    second = second.reshape(16, 64, 1024 - SPLIT)
    plus, minus = ring_shift("xz", 1), ring_shift("xz", -1)
    before = lax.ppermute(first, AXES, plus)
    after = lax.ppermute(first, AXES, minus)
    near = [lax.ppermute(second, AXES, ring_shift("yy", step)) for step in (1, -1)]
    lower, upper, got, second = forward_halves(before, after, (got, second), near)
    second = [second] + near + [lax.ppermute(second, AXES, ring_shift("yy", 2))]
    first = [
        first,
        before,
        after,
        lax.ppermute(lower, AXES, plus),
        lax.ppermute(upper, AXES, minus),
    ]

    got_other = sibling(got)
    meta_all = got[:, half + cols]
    ids = (meta_all[:, 0:32].astype(jnp.int32) * 256 + meta_all[:, 32:64].astype(jnp.int32)).reshape(256)
    maskf = meta_all[:, 64:96].astype(jnp.float32).reshape(256)
    ids_half = lax.dynamic_slice_in_dim(ids, core * half, half)
    mask_half = lax.dynamic_slice_in_dim(maskf, core * half, half)

    offsets = jnp.array(OFFSETS, jnp.int32)
    o1, o2, o3 = (
        offsets.reshape(shape) for shape in ((1, 1, 4), (1, 4, 1), (4, 1, 1))
    )
    zero = jnp.zeros((4, 4, 4), jnp.int32)

    def place(dx, dy, dz):
        px, py, pz = (x + dx) % 4, (y + dy) % 4, (z + dz) % 4
        return ((pz % 2 * 4 + px) * 8 + py * 2 + pz // 2 + zero).reshape(64)

    table = jnp.where(
        core == 0,
        jnp.stack([place(o3, o2, o1), place(o2, o3, o1)]),
        jnp.stack([place(o1, o2, o3), place(o1, o3, o2)]),
    )
    categories = jnp.arange(temps.shape[0], dtype=jnp.int32)
    taus = jnp.sum(
        jnp.where(variant_ids[:, None] == categories[None, :], temps[None, :], 0.0), axis=1
    )
    inv_tau = jnp.repeat(1.0 / taus, half)[None]

    base = jnp.stack([(b * 8 + a) * cols, ((b + 1 - 2 * core) * 8 + a) * cols])
    l_own, l_other, s_stats = student_logits(got, got_other, ids_half[None], base, cols)
    logits = (l_own, l_other)
    rows = jnp.arange(cols, dtype=jnp.int32)[:, None]
    onehots = [base[i] + rows == ids_half[None, :] for i in range(2)]

    e_own, e_other, stats = teacher_scores(
        table, inv_tau, first, second, (w_own, w_other), logits
    )
    e = (e_own, e_other)
    t_stats = stats[:3].reshape(24, half)
    packed = jnp.concatenate(
        [t_stats, s_stats]
    )
    def merge(g):
        n = g.shape[0]
        top = jnp.max(g[:, 0:8], axis=0)
        scale = jnp.exp(g[:, 0:8] - top)
        total = jnp.sum(g[:, 8:16] * scale, axis=0)
        cross = jnp.sum(g[:, 16:24] * scale, axis=0)
        stop = jnp.max(g[:, 24], axis=0)
        ssum = jnp.sum(g[:, 25] * jnp.exp(g[:, 24] - stop), axis=0)
        hard = jnp.sum(g[:, 26], axis=0)
        return jnp.concatenate(
            [top, total, cross, jnp.stack([stop, ssum, hard]), jnp.zeros((5, half), jnp.float32)]
        )

    tile8 = jnp.broadcast_to(packed[None], (8, 32, half))
    by_variant = merge(lax.all_to_all(tile8, "variant", 0, 0, tiled=True))
    tile16 = jnp.broadcast_to(by_variant[None], (16, 32, half))
    over = lax.all_to_all(tile16, "vocab", 0, 0, tiled=True).reshape(8, 2, 32, half)
    merged = merge(lax.dynamic_index_in_dim(over, core, 1, keepdims=False))
    top, total, cross = merged[0:8], merged[8:16], merged[16:24]
    lse = merged[24] + jnp.log(merged[25])
    hard = merged[26] - lse
    soft = jnp.sum(cross / total, axis=0) / 8 - lse
    loss_half = mask_half * (-mix_weight * soft - (1.0 - mix_weight) * hard)
    loss_all = ordered(core, loss_half, sibling(loss_half), 0)
    token_loss = lax.dynamic_slice_in_dim(loss_all, a * 32, 32)

    local_top = stats[0].reshape(8, half)
    coef = jnp.exp(local_top - top) / (8 * total)
    errors = []
    for i in range(2):
        averaged = sum(e[i][:, v * half : (v + 1) * half] * coef[v] for v in range(8))
        q = jnp.exp(logits[i] - lse)
        errors.append(
            (
                loss_scale
                * mask_half
                * (q - mix_weight * averaged - (1.0 - mix_weight) * onehots[i].astype(jnp.float32))
            ).astype(jnp.bfloat16)
        )
    error = ordered(core, errors[0], sibling(errors[1]), 1)
    error_all = lax.all_to_all(
        jnp.broadcast_to(error[None], (8, cols, 256)), "variant", 0, 0, tiled=True
    ).reshape(8 * cols, 256)
    grad_t = jnp.dot(error_all, student_hidden, preferred_element_type=jnp.float32)
    return token_loss, grad_t.T


def solution(mesh):
    in_specs = (
        P(None, None, ("variant", "vocab")),
        P(None, ("vocab", "variant")),
        P(),
        P(),
        P(None, "variant"),
        P("variant", "vocab"),
        P("variant"),
        P("variant"),
    )
    out_specs = (P("variant"), P("variant", "vocab"))
    return jax.shard_map(
        on_device, mesh=mesh, in_specs=in_specs, out_specs=out_specs, check_vma=False
    )
```

```python
import math
import jax
import jax.numpy as jnp
from jax import lax
from jax.experimental import pallas as pl
from jax.experimental.pallas import tpu as pltpu
from jax.sharding import PartitionSpec as P

mix_weight = 0.5
loss_scale = 4096.0

AXES = ("variant", "vocab")
SIDE = 4
ROWS = 640
OFFSETS = (0, -1, 1, 2)


def device_index(x, y, z, c):
    x, y, z = x % SIDE, y % SIDE, z % SIDE
    return ((z % 2) * SIDE + x) * 16 + y * 4 + (z // 2) * 2 + c


def permutation(move):
    return [
        (device_index(x, y, z, c), device_index(*move(x, y, z, c)))
        for x in range(SIDE)
        for y in range(SIDE)
        for z in range(SIDE)
        for c in range(2)
    ]


def ring_shift(axes, step):
    def move(x, y, z, c):
        at = {"x": x, "y": y, "z": z}
        at[axes[c]] += step
        return at["x"], at["y"], at["z"], c

    return permutation(move)


def sibling(value):
    return lax.ppermute(value, AXES, permutation(lambda x, y, z, c: (x, y, z, 1 - c)))


def ring_gather(value, axes):
    return [value] + [
        lax.ppermute(value, AXES, ring_shift(axes, step)) for step in (1, -1, 2)
    ]


def stack_kernel(*refs):
    for i in range(4):
        refs[-1][i] = refs[i][...]


def stack(blocks, after=()):
    vmem = pl.BlockSpec(memory_space=pltpu.VMEM)
    shape = (4,) + blocks[0].shape
    return pl.pallas_call(
        stack_kernel,
        out_shape=jax.ShapeDtypeStruct(shape, jnp.bfloat16),
        in_specs=[vmem] * 4 + [pl.BlockSpec(memory_space=pl.ANY)] * len(after),
        out_specs=vmem,
        cost_estimate=pl.CostEstimate(
            flops=0, bytes_accessed=4 * math.prod(shape), transcendentals=0
        ),
    )(*blocks, *after)


def halves_kernel(before, after, through_in, before_half, after_half, through_out):
    before_half[...] = before[...]
    after_half[...] = after[...]


def forward_halves(before, after, through):
    n, rows, lanes = before.shape
    block = (n // 2, rows, lanes)
    hbm = pl.BlockSpec(memory_space=pl.ANY)
    lower = pl.BlockSpec(block, lambda i: (0, 0, 0))
    return pl.pallas_call(
        halves_kernel,
        grid=(1,),
        out_shape=[jax.ShapeDtypeStruct(block, before.dtype)] * 2
        + [jax.ShapeDtypeStruct(through.shape, through.dtype)],
        in_specs=[lower, pl.BlockSpec(block, lambda i: (1, 0, 0)), hbm],
        out_specs=[lower, lower, hbm],
        input_output_aliases={2: 2},
        cost_estimate=pl.CostEstimate(
            flops=0, bytes_accessed=4 * n * rows * lanes, transcendentals=0
        ),
    )(before, after, through)


def copy_kernel(value, after, out, sem):
    copy = pltpu.make_async_copy(value, out, sem)
    copy.start()
    copy.wait()


def copy_after(value, after):
    hbm = pl.BlockSpec(memory_space=pl.ANY)
    return pl.pallas_call(
        copy_kernel,
        out_shape=jax.ShapeDtypeStruct(value.shape, value.dtype),
        in_specs=[hbm, hbm],
        out_specs=hbm,
        scratch_shapes=[pltpu.SemaphoreType.DMA(())],
        cost_estimate=pl.CostEstimate(
            flops=0, bytes_accessed=4 * math.prod(value.shape), transcendentals=0
        ),
    )(value, after)


def finish_kernel(g_ref, e_own, e_other, l_own, l_other, stat_ref, mask_ref, ids_ref, base_ref, *outs):
    err_refs, loss_ref = outs[0:2], outs[2]
    cols, half = l_own.shape
    near = g_ref[:, 0:8, :]
    top = jnp.max(near, axis=0)
    lse = top + jnp.log(jnp.sum(jnp.exp(near - top), axis=0))
    soft = jnp.sum(
        jnp.sum(jnp.exp(near - lse) * g_ref[:, 8:16, :], axis=0), axis=0, keepdims=True
    ) / 8
    students = g_ref[:, 16, :]
    s_top = jnp.max(students, axis=0, keepdims=True)
    s_lse = s_top + jnp.log(jnp.sum(jnp.exp(students - s_top), axis=0, keepdims=True))
    hard = jnp.sum(g_ref[:, 17, :], axis=0, keepdims=True) - s_lse
    mask = mask_ref[...]
    loss_ref[...] = mask * (-mix_weight * (soft - s_lse) - (1.0 - mix_weight) * hard)
    factors = [
        jnp.exp(stat_ref[2:3, v * half : (v + 1) * half] - lse[v : v + 1]) * (mix_weight / 8)
        for v in range(8)
    ]
    scale = loss_scale * mask
    rows = lax.broadcasted_iota(jnp.int32, (cols, half), 0)
    for i, (e, l) in enumerate(((e_own, l_own), (e_other, l_other))):
        value = jnp.exp(l[...] - s_lse)
        hit = rows + base_ref[i] == ids_ref[...]
        value -= jnp.where(hit, 1.0 - mix_weight, 0.0)
        averaged = e[:, 0:half] * factors[0]
        for v in range(1, 8):
            averaged += e[:, v * half : (v + 1) * half] * factors[v]
        err_refs[i][...] = (scale * (value - averaged)).astype(jnp.bfloat16)


def finish(gathered, e, logits, stats, mask, ids, base):
    cols, half = logits[0].shape
    vmem = pl.BlockSpec(memory_space=pltpu.VMEM)
    return pl.pallas_call(
        finish_kernel,
        out_shape=[
            jax.ShapeDtypeStruct((cols, half), jnp.bfloat16),
            jax.ShapeDtypeStruct((cols, half), jnp.bfloat16),
            jax.ShapeDtypeStruct((1, half), jnp.float32),
        ],
        in_specs=[vmem] * 8 + [pl.BlockSpec(memory_space=pltpu.SMEM)],
        out_specs=[vmem] * 3,
        compiler_params=pltpu.CompilerParams(vmem_limit_bytes=24 << 20),
        cost_estimate=pl.CostEstimate(
            flops=40 * cols * half, bytes_accessed=10 * cols * 1024, transcendentals=2 * cols * half
        ),
    )(gathered, *e, *logits, stats, mask, ids, base)


def student_kernel(own_ref, other_ref, ids_ref, base_ref, l_own, l_other, stat_ref):
    half, cols = l_own.shape[1], l_own.shape[0]
    dims = (((1,), (1,)), ((), ()))
    logits = []
    for ref, out in ((own_ref, l_own), (other_ref, l_other)):
        total = jnp.zeros((cols, half), jnp.float32)
        for block in range(8):
            total += lax.dot_general(
                ref[block, half : half + cols, :],
                own_ref[block, :half, :],
                dims,
                preferred_element_type=jnp.float32,
            )
        out[...] = total
        logits.append(total)
    top = jnp.maximum(
        jnp.max(logits[0], axis=0, keepdims=True), jnp.max(logits[1], axis=0, keepdims=True)
    )
    total = jnp.zeros((1, half), jnp.float32)
    hard = jnp.zeros((1, half), jnp.float32)
    rows = lax.broadcasted_iota(jnp.int32, (cols, half), 0)
    for i in range(2):
        total += jnp.sum(jnp.exp(logits[i] - top), axis=0, keepdims=True)
        hit = rows + base_ref[i] == ids_ref[...]
        hard += jnp.sum(jnp.where(hit, logits[i], 0.0), axis=0, keepdims=True)
    stat_ref[...] = jnp.concatenate([top + jnp.log(total), hard, jnp.zeros((6, half), jnp.float32)])


def student_logits(own, other, ids, base, cols):
    half = ids.shape[1]
    vmem = pl.BlockSpec(memory_space=pltpu.VMEM)
    return pl.pallas_call(
        student_kernel,
        out_shape=[
            jax.ShapeDtypeStruct((cols, half), jnp.float32),
            jax.ShapeDtypeStruct((cols, half), jnp.float32),
            jax.ShapeDtypeStruct((8, half), jnp.float32),
        ],
        in_specs=[vmem] * 3 + [pl.BlockSpec(memory_space=pltpu.SMEM)],
        out_specs=[vmem] * 3,
        compiler_params=pltpu.CompilerParams(vmem_limit_bytes=24 << 20),
        cost_estimate=pl.CostEstimate(
            flops=2 * 2 * cols * half * 2048, bytes_accessed=12 << 20, transcendentals=2 * cols * half
        ),
    )(own, other, ids, base)


def ordered(core, own, other, axis):
    return jnp.where(
        core == 0,
        jnp.concatenate([own, other], axis=axis),
        jnp.concatenate([other, own], axis=axis),
    )


def teacher_kernel(table, inv_tau, *refs):
    groups, w_refs, l_refs = refs[0:5], refs[5:7], refs[7:9]
    e_refs, stat_ref, hidden, sem = refs[9:11], refs[11], refs[12], refs[13]

    def chunk_copy(ref, base, n):
        row = pl.multiple_of(table[base + n] * 64, 64)
        return pltpu.make_async_copy(ref.at[n], hidden.at[pl.ds(row, 64)], sem)

    blocks = []
    base = 0
    for ref in groups:
        blocks.append((ref, base))
        base += ref.shape[0]
    for ref, base in blocks:
        def start(n, _, ref=ref, base=base):
            chunk_copy(ref, base, n).start()
            return 0
        lax.fori_loop(0, ref.shape[0], start, 0)
    for ref, base in blocks:
        def wait(n, _, ref=ref, base=base):
            chunk_copy(ref, base, n).wait()
            return 0
        lax.fori_loop(0, ref.shape[0], wait, 0)

    def tile(j, _):
        lanes = pl.ds(pl.multiple_of(j * 256, 256), 256)
        scale = inv_tau[:, lanes]
        block = hidden[:, lanes]
        scores = [
            jnp.dot(w[...], block, preferred_element_type=jnp.float32) * scale for w in w_refs
        ]
        top = jnp.maximum(
            jnp.max(scores[0], axis=0, keepdims=True), jnp.max(scores[1], axis=0, keepdims=True)
        )
        total = jnp.zeros((1, 256), jnp.float32)
        cross = jnp.zeros((1, 256), jnp.float32)
        for i in range(2):
            e = jnp.exp(scores[i] - top)
            e_refs[i][:, lanes] = e
            logits = l_refs[i][...]
            total += jnp.sum(e, axis=0, keepdims=True)
            cross += jnp.sum(
                e * jnp.concatenate([logits, logits], axis=1), axis=0, keepdims=True
            )
        stat_ref[0:1, lanes] = top + jnp.log(total)
        stat_ref[1:2, lanes] = cross / total
        stat_ref[2:3, lanes] = top
        return 0

    lax.fori_loop(0, 4, tile, 0)


def teacher_scores(table, inv_tau, hidden, weights, logits):
    cols, width = weights[0].shape
    vmem = pl.BlockSpec(memory_space=pltpu.VMEM)
    hbm = pl.BlockSpec(memory_space=pl.ANY)
    return pl.pallas_call(
        teacher_kernel,
        out_shape=[
            jax.ShapeDtypeStruct((cols, 1024), jnp.float32),
            jax.ShapeDtypeStruct((cols, 1024), jnp.float32),
            jax.ShapeDtypeStruct((8, 1024), jnp.float32),
        ],
        in_specs=[pl.BlockSpec(memory_space=pltpu.SMEM), vmem] + [hbm] * 5 + [vmem] * 4,
        out_specs=[vmem] * 3,
        scratch_shapes=[
            pltpu.VMEM((width, 1024), jnp.bfloat16),
            pltpu.SemaphoreType.DMA(()),
        ],
        compiler_params=pltpu.CompilerParams(vmem_limit_bytes=44 << 20),
        cost_estimate=pl.CostEstimate(
            flops=2 * 2 * cols * width * 1024,
            bytes_accessed=2 * (2 * cols * width + width * 1024) + 8 * cols * 1024,
            transcendentals=2 * cols * 1024,
        ),
    )(table, inv_tau, *hidden, *weights, *logits)


def on_device(
    teacher_hidden,
    teacher_weight,
    variant_ids,
    temps,
    student_hidden,
    student_weight,
    token_ids,
    loss_mask,
):
    a = lax.axis_index("variant")
    b = lax.axis_index("vocab")
    core = b % 2
    x, y, z = a % 4, b // 4, (b // 2) % 2 * 2 + a // 4
    cols = teacher_weight.shape[1]
    half = 128

    halves = [
        lax.dynamic_slice_in_dim(teacher_hidden, start * half, half, axis=1)
        .transpose(2, 0, 1)
        .reshape(32, 1024)
        for start in (core, 1 - core)
    ]
    unit = ordered(core, halves[0], sibling(halves[1]), 0)
    w_own = teacher_weight.T
    w_other = sibling(copy_after(w_own, unit))
    hidden = stack(ring_gather(unit, "zx"), (w_other,))

    meta = jnp.concatenate(
        [token_ids // 256, token_ids % 256, loss_mask, jnp.zeros((32,), jnp.int32)]
    ).astype(jnp.bfloat16)
    meta = jnp.concatenate([meta, hidden[0, 0, :128]])[None, None]
    mine = lax.dynamic_slice_in_dim(student_hidden, core * half, half, axis=0)
    send = jnp.concatenate(
        [
            jnp.broadcast_to(mine[None], (8, half, 256)),
            student_weight.T.reshape(8, cols, 256),
            jnp.broadcast_to(meta, (8, ROWS - half - cols, 256)),
        ],
        axis=1,
    )
    got = lax.all_to_all(send, "variant", 0, 0, tiled=True)

    hidden = stack(ring_gather(hidden, "yy")).reshape(16, 64, 1024)
    plus, minus = ring_shift("xz", 1), ring_shift("xz", -1)
    before = lax.ppermute(hidden, AXES, plus)
    after = lax.ppermute(hidden, AXES, minus)
    lower, upper, got = forward_halves(before, after, got)
    hidden = [
        hidden,
        before,
        after,
        lax.ppermute(lower, AXES, plus),
        lax.ppermute(upper, AXES, minus),
    ]

    got_other = sibling(got)
    meta_all = got[:, half + cols]
    ids = (meta_all[:, 0:32].astype(jnp.int32) * 256 + meta_all[:, 32:64].astype(jnp.int32)).reshape(256)
    maskf = meta_all[:, 64:96].astype(jnp.float32).reshape(256)
    ids_half = lax.dynamic_slice_in_dim(ids, core * half, half)
    mask_half = lax.dynamic_slice_in_dim(maskf, core * half, half)

    offsets = jnp.array(OFFSETS, jnp.int32)
    o1, o2, o3 = (
        offsets.reshape(shape) for shape in ((1, 1, 4), (1, 4, 1), (4, 1, 1))
    )
    zero = jnp.zeros((4, 4, 4), jnp.int32)

    def place(dx, dy, dz):
        px, py, pz = (x + dx) % 4, (y + dy) % 4, (z + dz) % 4
        return ((pz % 2 * 4 + px) * 8 + py * 2 + pz // 2 + zero).reshape(64)

    table = jnp.where(core == 0, place(o3, o2, o1), place(o1, o2, o3))
    categories = jnp.arange(temps.shape[0], dtype=jnp.int32)
    taus = jnp.sum(
        jnp.where(variant_ids[:, None] == categories[None, :], temps[None, :], 0.0), axis=1
    )
    inv_tau = jnp.repeat(1.0 / taus, half)[None]

    base = jnp.stack([(b * 8 + a) * cols, ((b + 1 - 2 * core) * 8 + a) * cols])
    l_own, l_other, s_stats = student_logits(got, got_other, ids_half[None], base, cols)
    logits = (l_own, l_other)
    e_own, e_other, stats = teacher_scores(
        table, inv_tau, hidden, (w_own, w_other), logits
    )
    packed = jnp.concatenate([stats[:2].reshape(16, half), s_stats])
    groups = [
        sorted(device_index(i // 16, i // 4, i, c) for i in range(64)) for c in range(2)
    ]
    gathered = lax.all_to_all(
        jnp.broadcast_to(packed[None], (64, 24, half)),
        AXES, 0, 0, tiled=True, axis_index_groups=groups,
    )
    *errors, loss_half = finish(
        gathered, (e_own, e_other), logits, stats, mask_half[None], ids_half[None], base
    )
    loss_half = loss_half[0]
    loss_all = ordered(core, loss_half, sibling(loss_half), 0)
    token_loss = lax.dynamic_slice_in_dim(loss_all, a * 32, 32)
    error = ordered(core, errors[0], sibling(errors[1]), 1)
    error_all = lax.all_to_all(
        jnp.broadcast_to(error[None], (8, cols, 256)), "variant", 0, 0, tiled=True
    ).reshape(8 * cols, 256)
    grad_t = jnp.dot(error_all, student_hidden, preferred_element_type=jnp.float32)
    return token_loss, grad_t.T


def solution(mesh):
    in_specs = (
        P(None, None, ("variant", "vocab")),
        P(None, ("vocab", "variant")),
        P(),
        P(),
        P(None, "variant"),
        P("variant", "vocab"),
        P("variant"),
        P("variant"),
    )
    out_specs = (P("variant"), P("variant", "vocab"))
    return jax.shard_map(
        on_device, mesh=mesh, in_specs=in_specs, out_specs=out_specs, check_vma=False
    )
```

```python
import functools
import math
import jax
import jax.numpy as jnp
from jax import lax
from jax.experimental import pallas as pl
from jax.experimental.pallas import tpu as pltpu
from jax.sharding import PartitionSpec as P

mix_weight = 0.5
loss_scale = 4096.0

AXES = ("variant", "vocab")
SIDE = 4
ROWS = 640
OFFSETS = (0, -1, 1, 2)


def device_index(x, y, z, c):
    x, y, z = x % SIDE, y % SIDE, z % SIDE
    return ((z % 2) * SIDE + x) * 16 + y * 4 + (z // 2) * 2 + c


def permutation(move):
    return [
        (device_index(x, y, z, c), device_index(*move(x, y, z, c)))
        for x in range(SIDE)
        for y in range(SIDE)
        for z in range(SIDE)
        for c in range(2)
    ]


def ring_shift(axes, step):
    def move(x, y, z, c):
        at = {"x": x, "y": y, "z": z}
        at[axes[c]] += step
        return at["x"], at["y"], at["z"], c

    return permutation(move)


def sibling(value):
    return lax.ppermute(value, AXES, permutation(lambda x, y, z, c: (x, y, z, 1 - c)))


def ring_gather(value, axes):
    return [value] + [
        lax.ppermute(value, AXES, ring_shift(axes, step)) for step in (1, -1, 2)
    ]


def stack_kernel(*refs):
    for i in range(4):
        if len(refs[i].shape) == 2:
            refs[-1][i] = refs[i][...]
        else:
            for j in range(4):
                refs[-1][4 * j + i] = refs[i][j]


def stack(blocks, after=()):
    vmem = pl.BlockSpec(memory_space=pltpu.VMEM)
    old = blocks[0].shape
    shape = (4,) + old if len(old) == 2 else (4 * old[0],) + old[1:]
    return pl.pallas_call(
        stack_kernel,
        out_shape=jax.ShapeDtypeStruct(shape, jnp.bfloat16),
        in_specs=[vmem] * 4 + [pl.BlockSpec(memory_space=pl.ANY)] * len(after),
        out_specs=vmem,
        cost_estimate=pl.CostEstimate(
            flops=0, bytes_accessed=4 * math.prod(shape), transcendentals=0
        ),
    )(*blocks, *after)


def halves_kernel(before, after, through_in, before_half, after_half, through_out):
    before_half[...] = before[...]
    after_half[...] = after[...]


def forward_halves(before, after, through):
    n, rows, lanes = before.shape
    block = (n // 2, rows, lanes)
    hbm = pl.BlockSpec(memory_space=pl.ANY)
    lower = pl.BlockSpec(block, lambda i: (0, 0, 0))
    return pl.pallas_call(
        halves_kernel,
        grid=(1,),
        out_shape=[jax.ShapeDtypeStruct(block, before.dtype)] * 2
        + [jax.ShapeDtypeStruct(through.shape, through.dtype)],
        in_specs=[lower, pl.BlockSpec(block, lambda i: (1, 0, 0)), hbm],
        out_specs=[lower, lower, hbm],
        input_output_aliases={2: 2},
        cost_estimate=pl.CostEstimate(
            flops=0, bytes_accessed=4 * n * rows * lanes, transcendentals=0
        ),
    )(before, after, through)


def reorder_kernel(w_ref, after, out_ref):
    step = pl.program_id(0)
    pairs = [w_ref[:, y * 128 : (y + 1) * 128] for y in range(SIDE)]
    for zh in range(2):
        for i in range(2):
            lane = pl.multiple_of(zh * 2048 + step * 256 + i * 128, 128)
            out_ref[:, pl.ds(lane, 128)] = jnp.concatenate(
                [pair[:, zh * 64 : (zh + 1) * 64] for pair in pairs[2 * i : 2 * i + 2]], axis=1
            )


def reorder(weight, after):
    cols, width = weight.shape
    return pl.pallas_call(
        reorder_kernel,
        grid=(8,),
        out_shape=jax.ShapeDtypeStruct((cols, width), weight.dtype),
        in_specs=[
            pl.BlockSpec((cols, 512), lambda i: (0, i)),
            pl.BlockSpec(memory_space=pl.ANY),
        ],
        out_specs=pl.BlockSpec((cols, width), lambda i: (0, 0)),
        cost_estimate=pl.CostEstimate(
            flops=0, bytes_accessed=4 * cols * width, transcendentals=0
        ),
    )(weight, after)


def finish_kernel(g_ref, e_own, e_other, l_own, l_other, stat_ref, mask_ref, ids_ref, base_ref, *outs):
    err_refs, loss_ref = outs[0:2], outs[2]
    cols, half = l_own.shape
    near = g_ref[:, 0:8, :]
    top = jnp.max(near, axis=0)
    lse = top + jnp.log(jnp.sum(jnp.exp(near - top), axis=0))
    soft = jnp.sum(
        jnp.sum(jnp.exp(near - lse) * g_ref[:, 8:16, :], axis=0), axis=0, keepdims=True
    ) / 8
    students = g_ref[:, 16, :]
    s_top = jnp.max(students, axis=0, keepdims=True)
    s_lse = s_top + jnp.log(jnp.sum(jnp.exp(students - s_top), axis=0, keepdims=True))
    hard = jnp.sum(g_ref[:, 17, :], axis=0, keepdims=True) - s_lse
    mask = mask_ref[...]
    loss_ref[...] = mask * (-mix_weight * (soft - s_lse) - (1.0 - mix_weight) * hard)
    factors = [
        jnp.exp(stat_ref[2:3, v * half : (v + 1) * half] - lse[v : v + 1]) * (mix_weight / 8)
        for v in range(8)
    ]
    scale = loss_scale * mask
    rows = lax.broadcasted_iota(jnp.int32, (cols, half), 0)
    for i, (e, l) in enumerate(((e_own, l_own), (e_other, l_other))):
        value = jnp.exp(l[...] - s_lse)
        hit = rows + base_ref[i] == ids_ref[...]
        value -= jnp.where(hit, 1.0 - mix_weight, 0.0)
        averaged = e[:, 0:half] * factors[0]
        for v in range(1, 8):
            averaged += e[:, v * half : (v + 1) * half] * factors[v]
        err_refs[i][...] = (scale * (value - averaged)).astype(jnp.bfloat16)


def finish(gathered, e, logits, stats, mask, ids, base):
    cols, half = logits[0].shape
    vmem = pl.BlockSpec(memory_space=pltpu.VMEM)
    return pl.pallas_call(
        finish_kernel,
        out_shape=[
            jax.ShapeDtypeStruct((cols, half), jnp.bfloat16),
            jax.ShapeDtypeStruct((cols, half), jnp.bfloat16),
            jax.ShapeDtypeStruct((1, half), jnp.float32),
        ],
        in_specs=[vmem] * 8 + [pl.BlockSpec(memory_space=pltpu.SMEM)],
        out_specs=[vmem] * 3,
        compiler_params=pltpu.CompilerParams(vmem_limit_bytes=24 << 20),
        cost_estimate=pl.CostEstimate(
            flops=40 * cols * half, bytes_accessed=10 * cols * 1024, transcendentals=2 * cols * half
        ),
    )(gathered, *e, *logits, stats, mask, ids, base)


def student_kernel(own_ref, other_ref, ids_ref, base_ref, l_own, l_other, stat_ref):
    half, cols = l_own.shape[1], l_own.shape[0]
    dims = (((1,), (1,)), ((), ()))
    logits = []
    for ref, out in ((own_ref, l_own), (other_ref, l_other)):
        total = jnp.zeros((cols, half), jnp.float32)
        for block in range(8):
            total += lax.dot_general(
                ref[block, half : half + cols, :],
                own_ref[block, :half, :],
                dims,
                preferred_element_type=jnp.float32,
            )
        out[...] = total
        logits.append(total)
    top = jnp.maximum(
        jnp.max(logits[0], axis=0, keepdims=True), jnp.max(logits[1], axis=0, keepdims=True)
    )
    total = jnp.zeros((1, half), jnp.float32)
    hard = jnp.zeros((1, half), jnp.float32)
    rows = lax.broadcasted_iota(jnp.int32, (cols, half), 0)
    for i in range(2):
        total += jnp.sum(jnp.exp(logits[i] - top), axis=0, keepdims=True)
        hit = rows + base_ref[i] == ids_ref[...]
        hard += jnp.sum(jnp.where(hit, logits[i], 0.0), axis=0, keepdims=True)
    stat_ref[...] = jnp.concatenate([top + jnp.log(total), hard, jnp.zeros((6, half), jnp.float32)])


def student_logits(own, other, ids, base, cols):
    half = ids.shape[1]
    vmem = pl.BlockSpec(memory_space=pltpu.VMEM)
    return pl.pallas_call(
        student_kernel,
        out_shape=[
            jax.ShapeDtypeStruct((cols, half), jnp.float32),
            jax.ShapeDtypeStruct((cols, half), jnp.float32),
            jax.ShapeDtypeStruct((8, half), jnp.float32),
        ],
        in_specs=[vmem] * 3 + [pl.BlockSpec(memory_space=pltpu.SMEM)],
        out_specs=[vmem] * 3,
        compiler_params=pltpu.CompilerParams(vmem_limit_bytes=24 << 20),
        cost_estimate=pl.CostEstimate(
            flops=2 * 2 * cols * half * 2048, bytes_accessed=12 << 20, transcendentals=2 * cols * half
        ),
    )(own, other, ids, base)


def ordered(core, own, other, axis):
    return jnp.where(
        core == 0,
        jnp.concatenate([own, other], axis=axis),
        jnp.concatenate([other, own], axis=axis),
    )


def gather_blocks(table, sources, w_refs, hidden, weights, sems):
    copies = []
    run = 0
    for ref, slot, first in sources:
        for s1 in range(first, first + ref.shape[0] // 4):
            at = run * 256
            for s2 in range(4):
                row = pl.multiple_of(at + table[16 + s2] * 64, 64)
                copies.append(
                    pltpu.make_async_copy(
                        ref.at[4 * (s1 - first) + s2], hidden.at[pl.ds(row, 64)], sems.at[0]
                    )
                )
            lane = pl.multiple_of(table[slot * 4 + s1] * 256, 256)
            for w, buf in zip(w_refs, weights):
                copies.append(
                    pltpu.make_async_copy(
                        w.at[:, pl.ds(lane, 256)], buf.at[:, pl.ds(at, 256)], sems.at[1]
                    )
                )
            run += 1
    for copy in copies:
        copy.start()
    for copy in copies:
        copy.wait()


def partial_kernel(sources, first, *refs):
    n = len(sources)
    table, w_refs = refs[0], refs[1 : 3]
    hidden_refs, refs = refs[3 : 3 + n], refs[3 + n :]
    olds = refs[:0] if first else refs[:2]
    outs = refs[len(olds) : len(olds) + 2]
    hidden, *weights, sems = refs[len(olds) + 2 :]
    gather_blocks(
        table, [(r,) + s for r, s in zip(hidden_refs, sources)], w_refs, hidden, weights, sems
    )

    def tile(j, _):
        lanes = pl.ds(pl.multiple_of(j * 256, 256), 256)
        block = hidden[:, lanes]
        for i in range(2):
            part = jnp.dot(weights[i][...], block, preferred_element_type=jnp.float32)
            outs[i][:, lanes] = part if first else olds[i][:, lanes] + part
        return 0

    lax.fori_loop(0, 4, tile, 0)


def last_kernel(sources, *refs):
    n = len(sources)
    table, inv_tau, w_refs = refs[0], refs[1], refs[2:4]
    hidden_refs, refs = refs[4 : 4 + n], refs[4 + n :]
    olds, l_refs, e_refs, stat_ref = refs[0:2], refs[2:4], refs[4:6], refs[6]
    hidden, *weights, sems = refs[7:]
    gather_blocks(
        table, [(r,) + s for r, s in zip(hidden_refs, sources)], w_refs, hidden, weights, sems
    )

    def tile(j, _):
        lanes = pl.ds(pl.multiple_of(j * 256, 256), 256)
        scale = inv_tau[:, lanes]
        block = hidden[:, lanes]
        scores = [
            (olds[i][:, lanes] + jnp.dot(weights[i][...], block, preferred_element_type=jnp.float32))
            * scale
            for i in range(2)
        ]
        top = jnp.maximum(
            jnp.max(scores[0], axis=0, keepdims=True), jnp.max(scores[1], axis=0, keepdims=True)
        )
        total = jnp.zeros((1, 256), jnp.float32)
        cross = jnp.zeros((1, 256), jnp.float32)
        for i in range(2):
            e = jnp.exp(scores[i] - top)
            e_refs[i][:, lanes] = e
            logits = l_refs[i][...]
            total += jnp.sum(e, axis=0, keepdims=True)
            cross += jnp.sum(
                e * jnp.concatenate([logits, logits], axis=1), axis=0, keepdims=True
            )
        stat_ref[0:1, lanes] = top + jnp.log(total)
        stat_ref[1:2, lanes] = cross / total
        stat_ref[2:3, lanes] = top
        return 0

    lax.fori_loop(0, 4, tile, 0)


def teacher_step(table, weights, hidden, sources, olds=(), last=()):
    cols = weights[0].shape[0]
    runs = sum(h.shape[0] for h in hidden) // 4
    smem = pl.BlockSpec(memory_space=pltpu.SMEM)
    vmem = pl.BlockSpec(memory_space=pltpu.VMEM)
    hbm = pl.BlockSpec(memory_space=pl.ANY)
    out_shape = [jax.ShapeDtypeStruct((cols, 1024), jnp.float32)] * 2
    if last:
        inv_tau, *logits = last
        body = functools.partial(last_kernel, sources)
        out_shape = out_shape + [jax.ShapeDtypeStruct((8, 1024), jnp.float32)]
        args = (table, inv_tau, *weights, *hidden, *olds, *logits)
        in_specs = [smem, vmem] + [hbm] * (2 + len(hidden)) + [vmem] * 4
    else:
        body = functools.partial(partial_kernel, sources, not olds)
        args = (table, *weights, *hidden, *olds)
        in_specs = [smem] + [hbm] * (2 + len(hidden)) + [vmem] * len(olds)
    return pl.pallas_call(
        body,
        out_shape=out_shape,
        in_specs=in_specs,
        out_specs=[vmem] * len(out_shape),
        scratch_shapes=[
            pltpu.VMEM((runs * 256, 1024), jnp.bfloat16),
            pltpu.VMEM((cols, runs * 256), jnp.bfloat16),
            pltpu.VMEM((cols, runs * 256), jnp.bfloat16),
            pltpu.SemaphoreType.DMA((2,)),
        ],
        compiler_params=pltpu.CompilerParams(vmem_limit_bytes=28 << 20),
        cost_estimate=pl.CostEstimate(
            flops=2 * 2 * cols * runs * 256 * 1024,
            bytes_accessed=2 * runs * 256 * (2 * cols + 1024) + 16 * cols * 1024,
            transcendentals=2 * cols * 1024 if last else 0,
        ),
    )(*args)


def on_device(
    teacher_hidden,
    teacher_weight,
    variant_ids,
    temps,
    student_hidden,
    student_weight,
    token_ids,
    loss_mask,
):
    a = lax.axis_index("variant")
    b = lax.axis_index("vocab")
    core = b % 2
    x, y, z = a % 4, b // 4, (b // 2) % 2 * 2 + a // 4
    cols = teacher_weight.shape[1]
    half = 128

    halves = [
        lax.dynamic_slice_in_dim(teacher_hidden, start * half, half, axis=1)
        .transpose(2, 0, 1)
        .reshape(32, 1024)
        for start in (core, 1 - core)
    ]
    unit = ordered(core, halves[0], sibling(halves[1]), 0)
    blocks = ring_gather(unit, "zx")
    w_own = reorder(teacher_weight.T, unit)
    w_other = sibling(w_own)
    weights = (w_own, w_other)

    meta = jnp.concatenate(
        [token_ids // 256, token_ids % 256, loss_mask, jnp.zeros((32,), jnp.int32)]
    ).astype(jnp.bfloat16)
    meta = jnp.concatenate([meta, unit[0, :128]])[None, None]
    mine = lax.dynamic_slice_in_dim(student_hidden, core * half, half, axis=0)
    send = jnp.concatenate(
        [
            jnp.broadcast_to(mine[None], (8, half, 256)),
            student_weight.T.reshape(8, cols, 256),
            jnp.broadcast_to(meta, (8, ROWS - half - cols, 256)),
        ],
        axis=1,
    )
    got = lax.all_to_all(send, "variant", 0, 0, tiled=True)

    hidden = stack(blocks, (send,))
    hidden = stack(ring_gather(hidden, "yy"))
    plus, minus = ring_shift("xz", 1), ring_shift("xz", -1)
    before = lax.ppermute(hidden, AXES, plus)
    after = lax.ppermute(hidden, AXES, minus)
    offsets = jnp.array(OFFSETS, jnp.int32)
    o1, o3 = offsets[None, :], offsets[:, None]
    px = (x + jnp.where(core == 0, o3, o1)) % 4
    pz = (z + jnp.where(core == 0, o1, o3)) % 4
    table = jnp.concatenate(
        [((pz // 2 * 2 + pz % 2) * 4 + px).reshape(16), (y + offsets) % 4]
    )
    lower, upper, got = forward_halves(before, after, got)
    partial = teacher_step(
        table, weights, (hidden, before, after), ((0, 0), (1, 0), (2, 0))
    )
    far = (lax.ppermute(lower, AXES, plus), lax.ppermute(upper, AXES, minus))

    got_other = sibling(got)
    meta_all = got[:, half + cols]
    ids = (meta_all[:, 0:32].astype(jnp.int32) * 256 + meta_all[:, 32:64].astype(jnp.int32)).reshape(256)
    maskf = meta_all[:, 64:96].astype(jnp.float32).reshape(256)
    ids_half = lax.dynamic_slice_in_dim(ids, core * half, half)
    mask_half = lax.dynamic_slice_in_dim(maskf, core * half, half)

    categories = jnp.arange(temps.shape[0], dtype=jnp.int32)
    taus = jnp.sum(
        jnp.where(variant_ids[:, None] == categories[None, :], temps[None, :], 0.0), axis=1
    )
    inv_tau = jnp.repeat(1.0 / taus, half)[None]

    base = jnp.stack([(b * 8 + a) * cols, ((b + 1 - 2 * core) * 8 + a) * cols])
    l_own, l_other, s_stats = student_logits(got, got_other, ids_half[None], base, cols)
    logits = (l_own, l_other)
    e_own, e_other, stats = teacher_step(
        table, weights, far, ((3, 0), (3, 2)), partial, (inv_tau, l_own, l_other)
    )
    packed = jnp.concatenate([stats[:2].reshape(16, half), s_stats])
    groups = [
        sorted(device_index(i // 16, i // 4, i, c) for i in range(64)) for c in range(2)
    ]
    gathered = lax.all_to_all(
        jnp.broadcast_to(packed[None], (64, 24, half)),
        AXES, 0, 0, tiled=True, axis_index_groups=groups,
    )
    *errors, loss_half = finish(
        gathered, (e_own, e_other), logits, stats, mask_half[None], ids_half[None], base
    )
    loss_half = loss_half[0]
    loss_all = ordered(core, loss_half, sibling(loss_half), 0)
    token_loss = lax.dynamic_slice_in_dim(loss_all, a * 32, 32)
    error = ordered(core, errors[0], sibling(errors[1]), 1)
    error_all = lax.all_to_all(
        jnp.broadcast_to(error[None], (8, cols, 256)), "variant", 0, 0, tiled=True
    ).reshape(8 * cols, 256)
    grad_t = jnp.dot(error_all, student_hidden, preferred_element_type=jnp.float32)
    return token_loss, grad_t.T


def solution(mesh):
    in_specs = (
        P(None, None, ("variant", "vocab")),
        P(None, ("vocab", "variant")),
        P(),
        P(),
        P(None, "variant"),
        P("variant", "vocab"),
        P("variant"),
        P("variant"),
    )
    out_specs = (P("variant"), P("variant", "vocab"))
    return jax.shard_map(
        on_device, mesh=mesh, in_specs=in_specs, out_specs=out_specs, check_vma=False
    )
```

```python
import functools
import math
import jax
import jax.numpy as jnp
from jax import lax
from jax.experimental import pallas as pl
from jax.experimental.pallas import tpu as pltpu
from jax.sharding import PartitionSpec as P

mix_weight = 0.5
loss_scale = 4096.0

AXES = ("variant", "vocab")
SIDE = 4
ROWS = 640
OFFSETS = (0, -1, 1, 2)


def device_index(x, y, z, c):
    x, y, z = x % SIDE, y % SIDE, z % SIDE
    return ((z % 2) * SIDE + x) * 16 + y * 4 + (z // 2) * 2 + c


def permutation(move):
    return [
        (device_index(x, y, z, c), device_index(*move(x, y, z, c)))
        for x in range(SIDE)
        for y in range(SIDE)
        for z in range(SIDE)
        for c in range(2)
    ]


def ring_shift(axes, step):
    def move(x, y, z, c):
        at = {"x": x, "y": y, "z": z}
        at[axes[c]] += step
        return at["x"], at["y"], at["z"], c

    return permutation(move)


def sibling(value):
    return lax.ppermute(value, AXES, permutation(lambda x, y, z, c: (x, y, z, 1 - c)))


def ring_gather(value, axes):
    return [value] + [
        lax.ppermute(value, AXES, ring_shift(axes, step)) for step in (1, -1, 2)
    ]


def stack_kernel(*refs):
    for i in range(4):
        if len(refs[i].shape) == 2:
            refs[-1][i] = refs[i][...]
        else:
            for j in range(4):
                refs[-1][4 * j + i] = refs[i][j]


def stack(blocks, after=()):
    vmem = pl.BlockSpec(memory_space=pltpu.VMEM)
    old = blocks[0].shape
    shape = (4,) + old if len(old) == 2 else (4 * old[0],) + old[1:]
    return pl.pallas_call(
        stack_kernel,
        out_shape=jax.ShapeDtypeStruct(shape, jnp.bfloat16),
        in_specs=[vmem] * 4 + [pl.BlockSpec(memory_space=pl.ANY)] * len(after),
        out_specs=vmem,
        cost_estimate=pl.CostEstimate(
            flops=0, bytes_accessed=4 * math.prod(shape), transcendentals=0
        ),
    )(*blocks, *after)


def halves_kernel(before, after, through_in, before_half, after_half, through_out):
    before_half[...] = before[...]
    after_half[...] = after[...]


def forward_halves(before, after, through):
    n, rows, lanes = before.shape
    block = (n // 2, rows, lanes)
    hbm = pl.BlockSpec(memory_space=pl.ANY)
    lower = pl.BlockSpec(block, lambda i: (0, 0, 0))
    return pl.pallas_call(
        halves_kernel,
        grid=(1,),
        out_shape=[jax.ShapeDtypeStruct(block, before.dtype)] * 2
        + [jax.ShapeDtypeStruct(through.shape, through.dtype)],
        in_specs=[lower, pl.BlockSpec(block, lambda i: (1, 0, 0)), hbm],
        out_specs=[lower, lower, hbm],
        input_output_aliases={2: 2},
        cost_estimate=pl.CostEstimate(
            flops=0, bytes_accessed=4 * n * rows * lanes, transcendentals=0
        ),
    )(before, after, through)


def reorder_kernel(w_ref, after, out_ref):
    step = pl.program_id(0)
    pairs = [w_ref[:, y * 128 : (y + 1) * 128] for y in range(SIDE)]
    for zh in range(2):
        for i in range(2):
            lane = pl.multiple_of(zh * 2048 + step * 256 + i * 128, 128)
            out_ref[:, pl.ds(lane, 128)] = jnp.concatenate(
                [pair[:, zh * 64 : (zh + 1) * 64] for pair in pairs[2 * i : 2 * i + 2]], axis=1
            )


def reorder(weight, after):
    cols, width = weight.shape
    return pl.pallas_call(
        reorder_kernel,
        grid=(8,),
        out_shape=jax.ShapeDtypeStruct((cols, width), weight.dtype),
        in_specs=[
            pl.BlockSpec((cols, 512), lambda i: (0, i)),
            pl.BlockSpec(memory_space=pl.ANY),
        ],
        out_specs=pl.BlockSpec((cols, width), lambda i: (0, 0)),
        cost_estimate=pl.CostEstimate(
            flops=0, bytes_accessed=4 * cols * width, transcendentals=0
        ),
    )(weight, after)


def finish_kernel(g_ref, e_ref, l_own, l_other, top_ref, mask_ref, ids_ref, base_ref, *outs):
    err_ref, loss_ref = outs
    cols, half = l_own.shape
    near = g_ref[:, 0:8, :]
    top = jnp.max(near, axis=0)
    lse = top + jnp.log(jnp.sum(jnp.exp(near - top), axis=0))
    soft = jnp.sum(
        jnp.sum(jnp.exp(near - lse) * g_ref[:, 8:16, :], axis=0), axis=0, keepdims=True
    ) / 8
    students = g_ref[:, 16, :]
    s_top = jnp.max(students, axis=0, keepdims=True)
    s_lse = s_top + jnp.log(jnp.sum(jnp.exp(students - s_top), axis=0, keepdims=True))
    hard = jnp.sum(g_ref[:, 17, :], axis=0, keepdims=True) - s_lse
    mask = mask_ref[...]
    loss_ref[...] = mask * (-mix_weight * (soft - s_lse) - (1.0 - mix_weight) * hard)
    factors = jnp.exp(top_ref[...] - lse) * (mix_weight / 8)
    scale = loss_scale * mask
    rows = lax.broadcasted_iota(jnp.int32, (cols, half), 0)
    core = base_ref[2]
    for i, l in enumerate((l_own, l_other)):
        value = jnp.exp(l[...] - s_lse)
        hit = rows + base_ref[i] == ids_ref[...]
        value -= jnp.where(hit, 1.0 - mix_weight, 0.0)
        averaged = e_ref[i, :, 0:half] * factors[0:1]
        for v in range(1, 8):
            averaged += e_ref[i, :, v * half : (v + 1) * half] * factors[v : v + 1]
        error = (scale * (value - averaged)).astype(jnp.bfloat16)
        target = core if i == 0 else 1 - core

        def spread(k, _, error=error, target=target):
            err_ref[2 * k + target] = error
            return 0

        lax.fori_loop(0, 8, spread, 0)


def finish(gathered, e, logits, top, mask, ids, base):
    cols, half = logits[0].shape
    vmem = pl.BlockSpec(memory_space=pltpu.VMEM)
    return pl.pallas_call(
        finish_kernel,
        out_shape=[
            jax.ShapeDtypeStruct((16, cols, half), jnp.bfloat16),
            jax.ShapeDtypeStruct((1, half), jnp.float32),
        ],
        in_specs=[vmem] * 7 + [pl.BlockSpec(memory_space=pltpu.SMEM)],
        out_specs=[vmem] * 2,
        compiler_params=pltpu.CompilerParams(vmem_limit_bytes=16 << 20),
        cost_estimate=pl.CostEstimate(
            flops=40 * cols * half, bytes_accessed=12 * cols * 1024, transcendentals=2 * cols * half
        ),
    )(gathered, e, *logits, top, mask, ids, base)


def grad_kernel(err_ref, hidden_ref, out_ref, rows_ref, sem):
    blocks, cols = err_ref.shape[0] // 2, err_ref.shape[1]
    copies, done = [], 0
    for k in range(blocks):
        error = jnp.concatenate([err_ref[2 * k], err_ref[2 * k + 1]], axis=1)
        rows_ref[k * cols : (k + 1) * cols, :] = jnp.dot(
            error, hidden_ref[...], preferred_element_type=jnp.float32
        )
        ready = (k + 1) * cols // 8 * 8
        here = pl.ds(done, ready - done)
        copies.append(pltpu.make_async_copy(rows_ref.at[here], out_ref.at[here], sem.at[k]))
        copies[-1].start()
        done = ready
    for copy in copies:
        copy.wait()


def student_gradient(errors, hidden):
    blocks, cols = errors.shape[0] // 2, errors.shape[1]
    vmem = pl.BlockSpec(memory_space=pltpu.VMEM)
    width = hidden.shape[1]
    return pl.pallas_call(
        grad_kernel,
        out_shape=jax.ShapeDtypeStruct((blocks * cols, width), jnp.float32),
        in_specs=[vmem, vmem],
        out_specs=pl.BlockSpec(memory_space=pltpu.HBM),
        scratch_shapes=[
            pltpu.VMEM((blocks * cols, width), jnp.float32),
            pltpu.SemaphoreType.DMA((blocks,)),
        ],
        compiler_params=pltpu.CompilerParams(vmem_limit_bytes=16 << 20),
        cost_estimate=pl.CostEstimate(
            flops=2 * blocks * cols * 256 * width, bytes_accessed=7 << 20, transcendentals=0
        ),
    )(errors, hidden)


def student_kernel(own_ref, other_ref, ids_ref, base_ref, l_own, l_other, stat_ref):
    half, cols = l_own.shape[1], l_own.shape[0]
    dims = (((1,), (1,)), ((), ()))
    logits = []
    for ref, out in ((own_ref, l_own), (other_ref, l_other)):
        total = jnp.zeros((cols, half), jnp.float32)
        for block in range(8):
            total += lax.dot_general(
                ref[block, half : half + cols, :],
                own_ref[block, :half, :],
                dims,
                preferred_element_type=jnp.float32,
            )
        out[...] = total
        logits.append(total)
    top = jnp.maximum(
        jnp.max(logits[0], axis=0, keepdims=True), jnp.max(logits[1], axis=0, keepdims=True)
    )
    total = jnp.zeros((1, half), jnp.float32)
    hard = jnp.zeros((1, half), jnp.float32)
    rows = lax.broadcasted_iota(jnp.int32, (cols, half), 0)
    for i in range(2):
        total += jnp.sum(jnp.exp(logits[i] - top), axis=0, keepdims=True)
        hit = rows + base_ref[i] == ids_ref[...]
        hard += jnp.sum(jnp.where(hit, logits[i], 0.0), axis=0, keepdims=True)
    stat_ref[...] = jnp.concatenate([top + jnp.log(total), hard, jnp.zeros((6, half), jnp.float32)])


def student_logits(own, other, ids, base, cols):
    half = ids.shape[1]
    vmem = pl.BlockSpec(memory_space=pltpu.VMEM)
    return pl.pallas_call(
        student_kernel,
        out_shape=[
            jax.ShapeDtypeStruct((cols, half), jnp.float32),
            jax.ShapeDtypeStruct((cols, half), jnp.float32),
            jax.ShapeDtypeStruct((8, half), jnp.float32),
        ],
        in_specs=[vmem] * 3 + [pl.BlockSpec(memory_space=pltpu.SMEM)],
        out_specs=[vmem] * 3,
        compiler_params=pltpu.CompilerParams(vmem_limit_bytes=24 << 20),
        cost_estimate=pl.CostEstimate(
            flops=2 * 2 * cols * half * 2048, bytes_accessed=12 << 20, transcendentals=2 * cols * half
        ),
    )(own, other, ids, base)


def ordered(core, own, other, axis):
    return jnp.where(
        core == 0,
        jnp.concatenate([own, other], axis=axis),
        jnp.concatenate([other, own], axis=axis),
    )


def gather_blocks(table, sources, w_refs, hidden, weights, sems):
    copies = []
    run = 0
    for ref, slot, first in sources:
        for s1 in range(first, first + ref.shape[0] // 4):
            at = run * 256
            for s2 in range(4):
                row = pl.multiple_of(at + table[16 + s2] * 64, 64)
                copies.append(
                    pltpu.make_async_copy(
                        ref.at[4 * (s1 - first) + s2], hidden.at[pl.ds(row, 64)], sems.at[0]
                    )
                )
            lane = pl.multiple_of(table[slot * 4 + s1] * 256, 256)
            for w, buf in zip(w_refs, weights):
                copies.append(
                    pltpu.make_async_copy(
                        w.at[:, pl.ds(lane, 256)], buf.at[:, pl.ds(at, 256)], sems.at[1]
                    )
                )
            run += 1
    for copy in copies:
        copy.start()
    for copy in copies:
        copy.wait()


def partial_kernel(sources, first, *refs):
    n = len(sources)
    table, w_refs = refs[0], refs[1 : 3]
    hidden_refs, refs = refs[3 : 3 + n], refs[3 + n :]
    olds = refs[:0] if first else refs[:2]
    outs = refs[len(olds) : len(olds) + 2]
    hidden, *weights, sems = refs[len(olds) + 2 :]
    gather_blocks(
        table, [(r,) + s for r, s in zip(hidden_refs, sources)], w_refs, hidden, weights, sems
    )

    def tile(j, _):
        lanes = pl.ds(pl.multiple_of(j * 256, 256), 256)
        block = hidden[:, lanes]
        for i in range(2):
            part = jnp.dot(weights[i][...], block, preferred_element_type=jnp.float32)
            outs[i][:, lanes] = part if first else olds[i][:, lanes] + part
        return 0

    lax.fori_loop(0, 4, tile, 0)


def last_kernel(sources, *refs):
    n = len(sources)
    table, inv_tau, w_refs = refs[0], refs[1], refs[2:4]
    hidden_refs, refs = refs[4 : 4 + n], refs[4 + n :]
    olds, l_refs, student = refs[0:2], refs[2:4], refs[4]
    e_ref, top_ref, stat_ref = refs[5:8]
    hidden, *weights, sems = refs[8:]
    gather_blocks(
        table, [(r,) + s for r, s in zip(hidden_refs, sources)], w_refs, hidden, weights, sems
    )
    for j in range(4):
        lanes = slice(j * 256, j * 256 + 256)
        scale = inv_tau[:, lanes]
        block = hidden[:, lanes]
        scores = [
            (olds[i][:, lanes] + jnp.dot(weights[i][...], block, preferred_element_type=jnp.float32))
            * scale
            for i in range(2)
        ]
        top = jnp.maximum(
            jnp.max(scores[0], axis=0, keepdims=True), jnp.max(scores[1], axis=0, keepdims=True)
        )
        total = jnp.zeros((1, 256), jnp.float32)
        cross = jnp.zeros((1, 256), jnp.float32)
        for i in range(2):
            e = jnp.exp(scores[i] - top)
            e_ref[i, :, lanes] = e
            logits = l_refs[i][...]
            total += jnp.sum(e, axis=0, keepdims=True)
            cross += jnp.sum(
                e * jnp.concatenate([logits, logits], axis=1), axis=0, keepdims=True
            )
        lse, mean = top + jnp.log(total), cross / total
        for k in range(2):
            part, v = slice(k * 128, k * 128 + 128), 2 * j + k
            top_ref[v : v + 1, :] = top[:, part]
            stat_ref[0, v : v + 1, :] = lse[:, part]
            stat_ref[0, 8 + v : 9 + v, :] = mean[:, part]
    stat_ref[0, 16:24, :] = student[...]
    rows = stat_ref[0]

    def spread(k, _):
        stat_ref[k] = rows
        return 0

    lax.fori_loop(1, stat_ref.shape[0], spread, 0)


def teacher_step(table, weights, hidden, sources, olds=(), last=()):
    cols = weights[0].shape[0]
    runs = sum(h.shape[0] for h in hidden) // 4
    smem = pl.BlockSpec(memory_space=pltpu.SMEM)
    vmem = pl.BlockSpec(memory_space=pltpu.VMEM)
    hbm = pl.BlockSpec(memory_space=pl.ANY)
    if last:
        inv_tau, *logits = last
        body = functools.partial(last_kernel, sources)
        out_shape = [
            jax.ShapeDtypeStruct((2, cols, 1024), jnp.float32),
            jax.ShapeDtypeStruct((8, 128), jnp.float32),
            jax.ShapeDtypeStruct((64, 24, 128), jnp.float32),
        ]
        args = (table, inv_tau, *weights, *hidden, *olds, *logits)
        in_specs = [smem, vmem] + [hbm] * (2 + len(hidden)) + [vmem] * 5
    else:
        out_shape = [jax.ShapeDtypeStruct((cols, 1024), jnp.float32)] * 2
        body = functools.partial(partial_kernel, sources, not olds)
        args = (table, *weights, *hidden, *olds)
        in_specs = [smem] + [hbm] * (2 + len(hidden)) + [vmem] * len(olds)
    return pl.pallas_call(
        body,
        out_shape=out_shape,
        in_specs=in_specs,
        out_specs=[vmem] * len(out_shape),
        scratch_shapes=[
            pltpu.VMEM((runs * 256, 1024), jnp.bfloat16),
            pltpu.VMEM((cols, runs * 256), jnp.bfloat16),
            pltpu.VMEM((cols, runs * 256), jnp.bfloat16),
            pltpu.SemaphoreType.DMA((2,)),
        ],
        compiler_params=pltpu.CompilerParams(vmem_limit_bytes=(50 if last else 56) << 20),
        cost_estimate=pl.CostEstimate(
            flops=2 * 2 * cols * runs * 256 * 1024,
            bytes_accessed=2 * runs * 256 * (2 * cols + 1024) + 16 * cols * 1024,
            transcendentals=2 * cols * 1024 if last else 0,
        ),
    )(*args)


def on_device(
    teacher_hidden,
    teacher_weight,
    variant_ids,
    temps,
    student_hidden,
    student_weight,
    token_ids,
    loss_mask,
):
    a = lax.axis_index("variant")
    b = lax.axis_index("vocab")
    core = b % 2
    x, y, z = a % 4, b // 4, (b // 2) % 2 * 2 + a // 4
    cols = teacher_weight.shape[1]
    half = 128

    halves = [
        lax.dynamic_slice_in_dim(teacher_hidden, start * half, half, axis=1)
        .transpose(2, 0, 1)
        .reshape(32, 1024)
        for start in (core, 1 - core)
    ]
    unit = ordered(core, halves[0], sibling(halves[1]), 0)
    blocks = ring_gather(unit, "zx")
    w_own = reorder(teacher_weight.T, unit)
    w_other = sibling(w_own)
    weights = (w_own, w_other)

    meta = jnp.concatenate(
        [token_ids // 256, token_ids % 256, loss_mask, jnp.zeros((32,), jnp.int32)]
    ).astype(jnp.bfloat16)
    meta = jnp.concatenate([meta, unit[0, :128]])[None, None]
    mine = lax.dynamic_slice_in_dim(student_hidden, core * half, half, axis=0)
    send = jnp.concatenate(
        [
            jnp.broadcast_to(mine[None], (8, half, 256)),
            student_weight.T.reshape(8, cols, 256),
            jnp.broadcast_to(meta, (8, ROWS - half - cols, 256)),
        ],
        axis=1,
    )
    got = lax.all_to_all(send, "variant", 0, 0, tiled=True)

    hidden = stack(blocks, (send,))
    hidden = stack(ring_gather(hidden, "yy"))
    plus, minus = ring_shift("xz", 1), ring_shift("xz", -1)
    before = lax.ppermute(hidden, AXES, plus)
    after = lax.ppermute(hidden, AXES, minus)
    offsets = jnp.array(OFFSETS, jnp.int32)
    o1, o3 = offsets[None, :], offsets[:, None]
    px = (x + jnp.where(core == 0, o3, o1)) % 4
    pz = (z + jnp.where(core == 0, o1, o3)) % 4
    table = jnp.concatenate(
        [((pz // 2 * 2 + pz % 2) * 4 + px).reshape(16), (y + offsets) % 4]
    )
    lower, upper, got = forward_halves(before, after, got)
    partial = teacher_step(
        table, weights, (hidden, before, after), ((0, 0), (1, 0), (2, 0))
    )
    far = (lax.ppermute(lower, AXES, plus), lax.ppermute(upper, AXES, minus))

    got_other = sibling(got)
    meta_all = got[:, half + cols]
    ids = (meta_all[:, 0:32].astype(jnp.int32) * 256 + meta_all[:, 32:64].astype(jnp.int32)).reshape(256)
    maskf = meta_all[:, 64:96].astype(jnp.float32).reshape(256)
    ids_half = lax.dynamic_slice_in_dim(ids, core * half, half)
    mask_half = lax.dynamic_slice_in_dim(maskf, core * half, half)

    categories = jnp.arange(temps.shape[0], dtype=jnp.int32)
    taus = jnp.sum(
        jnp.where(variant_ids[:, None] == categories[None, :], temps[None, :], 0.0), axis=1
    )
    inv_tau = jnp.repeat(1.0 / taus, half)[None]

    base = jnp.stack([(b * 8 + a) * cols, ((b + 1 - 2 * core) * 8 + a) * cols])
    l_own, l_other, s_stats = student_logits(got, got_other, ids_half[None], base, cols)
    logits = (l_own, l_other)
    e, local_top, packed = teacher_step(
        table, weights, far, ((3, 0), (3, 2)), partial, (inv_tau, l_own, l_other, s_stats)
    )
    groups = [
        sorted(device_index(i // 16, i // 4, i, c) for i in range(64)) for c in range(2)
    ]
    gathered = lax.all_to_all(packed, AXES, 0, 0, tiled=True, axis_index_groups=groups)
    errors, loss_half = finish(
        gathered, e, logits, local_top, mask_half[None], ids_half[None],
        jnp.concatenate([base, core[None]]),
    )
    loss_half = loss_half[0]
    loss_all = ordered(core, loss_half, sibling(loss_half), 0)
    token_loss = lax.dynamic_slice_in_dim(loss_all, a * 32, 32)
    pairs = [[v * 16 + 2 * k + c for v in range(8) for c in range(2)] for k in range(8)]
    errors = lax.all_to_all(errors, AXES, 0, 0, tiled=True, axis_index_groups=pairs)
    return token_loss, student_gradient(errors, student_hidden).T


def solution(mesh):
    in_specs = (
        P(None, None, ("variant", "vocab")),
        P(None, ("vocab", "variant")),
        P(),
        P(),
        P(None, "variant"),
        P("variant", "vocab"),
        P("variant"),
        P("variant"),
    )
    out_specs = (P("variant"), P("variant", "vocab"))
    return jax.shard_map(
        on_device, mesh=mesh, in_specs=in_specs, out_specs=out_specs, check_vma=False
    )
```

```python
import functools
import math
import jax
import jax.numpy as jnp
from jax import lax
from jax.experimental import pallas as pl
from jax.experimental.pallas import tpu as pltpu
from jax.sharding import PartitionSpec as P

mix_weight = 0.5
loss_scale = 4096.0

AXES = ("variant", "vocab")
SIDE = 4
ROWS = 640
OFFSETS = (0, -1, 1, 2)


def device_index(x, y, z, c):
    x, y, z = x % SIDE, y % SIDE, z % SIDE
    return ((z % 2) * SIDE + x) * 16 + y * 4 + (z // 2) * 2 + c


def permutation(move):
    return [
        (device_index(x, y, z, c), device_index(*move(x, y, z, c)))
        for x in range(SIDE)
        for y in range(SIDE)
        for z in range(SIDE)
        for c in range(2)
    ]


def ring_shift(axes, step):
    def move(x, y, z, c):
        at = {"x": x, "y": y, "z": z}
        at[axes[c]] += step
        return at["x"], at["y"], at["z"], c

    return permutation(move)


def sibling(value):
    return lax.ppermute(value, AXES, permutation(lambda x, y, z, c: (x, y, z, 1 - c)))


def ring_gather(value, axes):
    return [value] + [
        lax.ppermute(value, AXES, ring_shift(axes, step)) for step in (1, -1, 2)
    ]


def stack_kernel(*refs):
    for i in range(4):
        if len(refs[i].shape) == 2:
            refs[-1][i] = refs[i][...]
        else:
            for j in range(4):
                refs[-1][4 * j + i] = refs[i][j]


def stack(blocks, after=()):
    vmem = pl.BlockSpec(memory_space=pltpu.VMEM)
    old = blocks[0].shape
    shape = (4,) + old if len(old) == 2 else (4 * old[0],) + old[1:]
    return pl.pallas_call(
        stack_kernel,
        out_shape=jax.ShapeDtypeStruct(shape, jnp.bfloat16),
        in_specs=[vmem] * 4 + [pl.BlockSpec(memory_space=pl.ANY)] * len(after),
        out_specs=vmem,
        cost_estimate=pl.CostEstimate(
            flops=0, bytes_accessed=4 * math.prod(shape), transcendentals=0
        ),
    )(*blocks, *after)


def halves_kernel(before, after, through_in, other, before_half, after_half, through_out):
    before_half[...] = before[...]
    after_half[...] = after[...]


def forward_halves(before, after, through, other):
    n, rows, lanes = before.shape
    block = (n // 2, rows, lanes)
    hbm = pl.BlockSpec(memory_space=pl.ANY)
    lower = pl.BlockSpec(block, lambda i: (0, 0, 0))
    return pl.pallas_call(
        halves_kernel,
        grid=(1,),
        out_shape=[jax.ShapeDtypeStruct(block, before.dtype)] * 2
        + [jax.ShapeDtypeStruct(through.shape, through.dtype)],
        in_specs=[lower, pl.BlockSpec(block, lambda i: (1, 0, 0)), hbm, hbm],
        out_specs=[lower, lower, hbm],
        input_output_aliases={2: 2},
        cost_estimate=pl.CostEstimate(
            flops=0, bytes_accessed=4 * n * rows * lanes, transcendentals=0
        ),
    )(before, after, through, other)


def reorder_kernel(w_ref, after, *out_refs):
    step = pl.program_id(0)
    cols = w_ref.shape[0]
    pairs = [w_ref[:, y * 128 : (y + 1) * 128] for y in range(SIDE)]
    for zh in range(2):
        for i in range(2):
            lane = pl.multiple_of(zh * 2048 + step * 256 + i * 128, 128)
            piece = jnp.concatenate(
                [pair[:, zh * 64 : (zh + 1) * 64] for pair in pairs[2 * i : 2 * i + 2]], axis=1
            )
            for k, out_ref in enumerate(out_refs):
                here = piece[128 * k : min(128 * (k + 1), cols)]
                out_ref[: here.shape[0], pl.ds(lane, 128)] = here


def reorder(weight, after):
    cols, width = weight.shape
    return pl.pallas_call(
        reorder_kernel,
        grid=(8,),
        out_shape=[jax.ShapeDtypeStruct((128, width), weight.dtype)] * 4,
        in_specs=[
            pl.BlockSpec((cols, 512), lambda i: (0, i)),
            pl.BlockSpec(memory_space=pl.ANY),
        ],
        out_specs=[pl.BlockSpec((128, width), lambda i: (0, 0))] * 4,
        cost_estimate=pl.CostEstimate(
            flops=0, bytes_accessed=4 * cols * width, transcendentals=0
        ),
    )(weight, after)


def finish_kernel(g_ref, e_ref, l_own, l_other, top_ref, mask_ref, ids_ref, base_ref, *outs):
    err_ref, loss_ref = outs
    cols, half = l_own.shape
    near = g_ref[:, 0:8, :]
    top = jnp.max(near, axis=0)
    lse = top + jnp.log(jnp.sum(jnp.exp(near - top), axis=0))
    soft = jnp.sum(
        jnp.sum(jnp.exp(near - lse) * g_ref[:, 8:16, :], axis=0), axis=0, keepdims=True
    ) / 8
    students = g_ref[:, 16, :]
    s_top = jnp.max(students, axis=0, keepdims=True)
    s_lse = s_top + jnp.log(jnp.sum(jnp.exp(students - s_top), axis=0, keepdims=True))
    hard = jnp.sum(g_ref[:, 17, :], axis=0, keepdims=True) - s_lse
    mask = mask_ref[...]
    loss_ref[...] = mask * (-mix_weight * (soft - s_lse) - (1.0 - mix_weight) * hard)
    factors = jnp.exp(top_ref[...] - lse) * (mix_weight / 8)
    scale = loss_scale * mask
    rows = lax.broadcasted_iota(jnp.int32, (cols, half), 0)
    core = base_ref[2]
    for i, l in enumerate((l_own, l_other)):
        value = jnp.exp(l[...] - s_lse)
        hit = rows + base_ref[i] == ids_ref[...]
        value -= jnp.where(hit, 1.0 - mix_weight, 0.0)
        averaged = e_ref[i, :, 0:half] * factors[0:1]
        for v in range(1, 8):
            averaged += e_ref[i, :, v * half : (v + 1) * half] * factors[v : v + 1]
        error = (scale * (value - averaged)).astype(jnp.bfloat16)
        target = core if i == 0 else 1 - core

        def spread(k, _, error=error, target=target):
            err_ref[2 * k + target] = error
            return 0

        lax.fori_loop(0, 8, spread, 0)


def finish(gathered, e, logits, top, mask, ids, base):
    cols, half = logits[0].shape
    vmem = pl.BlockSpec(memory_space=pltpu.VMEM)
    return pl.pallas_call(
        finish_kernel,
        out_shape=[
            jax.ShapeDtypeStruct((16, cols, half), jnp.bfloat16),
            jax.ShapeDtypeStruct((1, half), jnp.float32),
        ],
        in_specs=[vmem] * 7 + [pl.BlockSpec(memory_space=pltpu.SMEM)],
        out_specs=[vmem] * 2,
        compiler_params=pltpu.CompilerParams(vmem_limit_bytes=16 << 20),
        cost_estimate=pl.CostEstimate(
            flops=40 * cols * half, bytes_accessed=12 * cols * 1024, transcendentals=2 * cols * half
        ),
    )(gathered, e, *logits, top, mask, ids, base)


def grad_kernel(err_ref, hidden_ref, out_ref, rows_ref, sem):
    blocks, cols = err_ref.shape[0] // 2, err_ref.shape[1]
    copies, done = [], 0
    for k in range(blocks):
        error = jnp.concatenate([err_ref[2 * k], err_ref[2 * k + 1]], axis=1)
        rows_ref[k * cols : (k + 1) * cols, :] = jnp.dot(
            error, hidden_ref[...], preferred_element_type=jnp.float32
        )
        ready = (k + 1) * cols // 8 * 8
        here = pl.ds(done, ready - done)
        copies.append(pltpu.make_async_copy(rows_ref.at[here], out_ref.at[here], sem.at[k]))
        copies[-1].start()
        done = ready
    for copy in copies:
        copy.wait()


def student_gradient(errors, hidden):
    blocks, cols = errors.shape[0] // 2, errors.shape[1]
    vmem = pl.BlockSpec(memory_space=pltpu.VMEM)
    width = hidden.shape[1]
    return pl.pallas_call(
        grad_kernel,
        out_shape=jax.ShapeDtypeStruct((blocks * cols, width), jnp.float32),
        in_specs=[vmem, vmem],
        out_specs=pl.BlockSpec(memory_space=pltpu.HBM),
        scratch_shapes=[
            pltpu.VMEM((blocks * cols, width), jnp.float32),
            pltpu.SemaphoreType.DMA((blocks,)),
        ],
        compiler_params=pltpu.CompilerParams(vmem_limit_bytes=16 << 20),
        cost_estimate=pl.CostEstimate(
            flops=2 * blocks * cols * 256 * width, bytes_accessed=7 << 20, transcendentals=0
        ),
    )(errors, hidden)


def student_kernel(own_ref, other_ref, ids_ref, base_ref, l_own, l_other, stat_ref):
    half, cols = l_own.shape[1], l_own.shape[0]
    dims = (((1,), (1,)), ((), ()))
    logits = []
    for ref, out in ((own_ref, l_own), (other_ref, l_other)):
        total = jnp.zeros((cols, half), jnp.float32)
        for block in range(8):
            total += lax.dot_general(
                ref[block, half : half + cols, :],
                own_ref[block, :half, :],
                dims,
                preferred_element_type=jnp.float32,
            )
        out[...] = total
        logits.append(total)
    top = jnp.maximum(
        jnp.max(logits[0], axis=0, keepdims=True), jnp.max(logits[1], axis=0, keepdims=True)
    )
    total = jnp.zeros((1, half), jnp.float32)
    hard = jnp.zeros((1, half), jnp.float32)
    rows = lax.broadcasted_iota(jnp.int32, (cols, half), 0)
    for i in range(2):
        total += jnp.sum(jnp.exp(logits[i] - top), axis=0, keepdims=True)
        hit = rows + base_ref[i] == ids_ref[...]
        hard += jnp.sum(jnp.where(hit, logits[i], 0.0), axis=0, keepdims=True)
    stat_ref[...] = jnp.concatenate([top + jnp.log(total), hard, jnp.zeros((6, half), jnp.float32)])


def student_logits(own, other, ids, base, cols):
    half = ids.shape[1]
    vmem = pl.BlockSpec(memory_space=pltpu.VMEM)
    return pl.pallas_call(
        student_kernel,
        out_shape=[
            jax.ShapeDtypeStruct((cols, half), jnp.float32),
            jax.ShapeDtypeStruct((cols, half), jnp.float32),
            jax.ShapeDtypeStruct((8, half), jnp.float32),
        ],
        in_specs=[vmem] * 3 + [pl.BlockSpec(memory_space=pltpu.SMEM)],
        out_specs=[vmem] * 3,
        compiler_params=pltpu.CompilerParams(vmem_limit_bytes=24 << 20),
        cost_estimate=pl.CostEstimate(
            flops=2 * 2 * cols * half * 2048, bytes_accessed=12 << 20, transcendentals=2 * cols * half
        ),
    )(own, other, ids, base)


def ordered(core, own, other, axis):
    return jnp.where(
        core == 0,
        jnp.concatenate([own, other], axis=axis),
        jnp.concatenate([other, own], axis=axis),
    )


def gather_blocks(table, sources, w_refs, hidden, weights, sems):
    copies = []
    run = 0
    for ref, slot, first in sources:
        for s1 in range(first, first + ref.shape[0] // 4):
            at = run * 256
            for s2 in range(4):
                row = pl.multiple_of(at + table[16 + s2] * 64, 64)
                copies.append(
                    pltpu.make_async_copy(
                        ref.at[4 * (s1 - first) + s2], hidden.at[pl.ds(row, 64)], sems.at[0]
                    )
                )
            lane = pl.multiple_of(table[slot * 4 + s1] * 256, 256)
            for k, w in enumerate(w_refs):
                copies.append(
                    pltpu.make_async_copy(
                        w.at[:, pl.ds(lane, 256)],
                        weights.at[pl.ds(128 * k, 128), pl.ds(at, 256)],
                        sems.at[1],
                    )
                )
            run += 1
    for copy in copies:
        copy.start()
    for copy in copies:
        copy.wait()


def partial_kernel(sources, first, *refs):
    n = len(sources)
    table, w_refs, hidden_refs, refs = refs[0], refs[1:9], refs[9 : 9 + n], refs[9 + n :]
    old = None if first else refs[0]
    hidden, weights, sems = refs[-3:]
    out, done = refs[0 if first else 1], refs[1 if first else 2]
    gather_blocks(
        table, [(r,) + s for r, s in zip(hidden_refs, sources)], w_refs, hidden, weights, sems
    )
    done[...] = jnp.zeros_like(done)

    def tile(j, _):
        lanes = pl.ds(pl.multiple_of(j * 256, 256), 256)
        part = jnp.dot(weights[...], hidden[:, lanes], preferred_element_type=jnp.float32)
        out[:, lanes] = part if first else old[:, lanes] + part
        return 0

    lax.fori_loop(0, 4, tile, 0)


def last_kernel(sources, *refs):
    n = len(sources)
    table, inv_tau, w_refs = refs[0], refs[1], refs[2:10]
    hidden_refs, refs = refs[10 : 10 + n], refs[10 + n :]
    old, l_refs, student = refs[0], refs[1:3], refs[3]
    e_ref, top_ref, stat_ref = refs[4:7]
    hidden, weights, sems = refs[7:]
    cols = e_ref.shape[1]
    gather_blocks(
        table, [(r,) + s for r, s in zip(hidden_refs, sources)], w_refs, hidden, weights, sems
    )
    for j in range(4):
        lanes = slice(j * 256, j * 256 + 256)
        scale = inv_tau[:, lanes]
        part = jnp.dot(weights[...], hidden[:, lanes], preferred_element_type=jnp.float32)
        scores = [
            (old[i * 512 : i * 512 + cols, lanes] + part[i * 512 : i * 512 + cols]) * scale
            for i in range(2)
        ]
        top = jnp.maximum(
            jnp.max(scores[0], axis=0, keepdims=True), jnp.max(scores[1], axis=0, keepdims=True)
        )
        total = jnp.zeros((1, 256), jnp.float32)
        cross = jnp.zeros((1, 256), jnp.float32)
        for i in range(2):
            e = jnp.exp(scores[i] - top)
            e_ref[i, :, lanes] = e
            logits = l_refs[i][...]
            total += jnp.sum(e, axis=0, keepdims=True)
            cross += jnp.sum(
                e * jnp.concatenate([logits, logits], axis=1), axis=0, keepdims=True
            )
        lse, mean = top + jnp.log(total), cross / total
        for k in range(2):
            part, v = slice(k * 128, k * 128 + 128), 2 * j + k
            top_ref[v : v + 1, :] = top[:, part]
            stat_ref[0, v : v + 1, :] = lse[:, part]
            stat_ref[0, 8 + v : 9 + v, :] = mean[:, part]
    stat_ref[0, 16:24, :] = student[...]
    rows = stat_ref[0]

    def spread(k, _):
        stat_ref[k] = rows
        return 0

    lax.fori_loop(1, stat_ref.shape[0], spread, 0)


def teacher_step(table, weights, hidden, sources, cols, old=(), last=()):
    width = weights[0].shape[1]
    runs = sum(h.shape[0] for h in hidden) // 4
    smem = pl.BlockSpec(memory_space=pltpu.SMEM)
    vmem = pl.BlockSpec(memory_space=pltpu.VMEM)
    hbm = pl.BlockSpec(memory_space=pltpu.HBM)
    if last:
        inv_tau, *student = last
        body = functools.partial(last_kernel, sources)
        out_shape = [
            jax.ShapeDtypeStruct((2, cols, 1024), jnp.float32),
            jax.ShapeDtypeStruct((8, 128), jnp.float32),
            jax.ShapeDtypeStruct((64, 24, 128), jnp.float32),
        ]
        args = (table, inv_tau, *weights, *hidden, *old, *student)
        in_specs = [smem, vmem] + [hbm] * (8 + len(hidden)) + [vmem] * 4
        out_specs = [vmem] * 3
    else:
        body = functools.partial(partial_kernel, sources, not old)
        out_shape = [
            jax.ShapeDtypeStruct((1024, 1024), jnp.float32),
            jax.ShapeDtypeStruct((8, 128), jnp.float32),
        ]
        args = (table, *weights, *hidden, *old)
        in_specs = [smem] + [hbm] * (8 + len(hidden)) + [vmem] * len(old)
        out_specs = [vmem] * 2
    return pl.pallas_call(
        body,
        out_shape=out_shape,
        in_specs=in_specs,
        out_specs=out_specs,
        scratch_shapes=[
            pltpu.VMEM((runs * 256, 1024), jnp.bfloat16),
            pltpu.VMEM((1024, runs * 256), jnp.bfloat16),
            pltpu.SemaphoreType.DMA((2,)),
        ],
        compiler_params=pltpu.CompilerParams(vmem_limit_bytes=(52 if last else 56) << 20),
        cost_estimate=pl.CostEstimate(
            flops=2 * 1024 * runs * 256 * 1024 if last else 100 << 20,
            bytes_accessed=8 << 20 if last else 100 << 10,
            transcendentals=2 * cols * 1024 if last else 0,
        ),
    )(*args)


def on_device(
    teacher_hidden,
    teacher_weight,
    variant_ids,
    temps,
    student_hidden,
    student_weight,
    token_ids,
    loss_mask,
):
    a = lax.axis_index("variant")
    b = lax.axis_index("vocab")
    core = b % 2
    x, y, z = a % 4, b // 4, (b // 2) % 2 * 2 + a // 4
    cols = teacher_weight.shape[1]
    half = 128

    halves = [
        lax.dynamic_slice_in_dim(teacher_hidden, start * half, half, axis=1)
        .transpose(2, 0, 1)
        .reshape(32, 1024)
        for start in (core, 1 - core)
    ]
    unit = ordered(core, halves[0], sibling(halves[1]), 0)
    blocks = ring_gather(unit, "zx")

    meta = jnp.concatenate(
        [token_ids // 256, token_ids % 256, loss_mask, jnp.zeros((32,), jnp.int32)]
    ).astype(jnp.bfloat16)
    meta = jnp.concatenate([meta, unit[0, :128]])[None, None]
    mine = lax.dynamic_slice_in_dim(student_hidden, core * half, half, axis=0)
    send = jnp.concatenate(
        [
            jnp.broadcast_to(mine[None], (8, half, 256)),
            student_weight.T.reshape(8, cols, 256),
            jnp.broadcast_to(meta, (8, ROWS - half - cols, 256)),
        ],
        axis=1,
    )
    got = lax.all_to_all(send, "variant", 0, 0, tiled=True)

    hidden = stack(blocks, (send,))
    hidden = stack(ring_gather(hidden, "yy"))
    w_own = reorder(teacher_weight.T, unit)
    weights = (*w_own, *(sibling(w) for w in w_own))
    plus, minus = ring_shift("xz", 1), ring_shift("xz", -1)
    before = lax.ppermute(hidden, AXES, plus)
    after = lax.ppermute(hidden, AXES, minus)
    offsets = jnp.array(OFFSETS, jnp.int32)
    o1, o3 = offsets[None, :], offsets[:, None]
    px = (x + jnp.where(core == 0, o3, o1)) % 4
    pz = (z + jnp.where(core == 0, o1, o3)) % 4
    table = jnp.concatenate(
        [((pz // 2 * 2 + pz % 2) * 4 + px).reshape(16), (y + offsets) % 4]
    )
    partial, done = teacher_step(table, weights, (hidden,), ((0, 0),), cols)
    lower, upper, got = forward_halves(before, after, got, done)
    partial, done = teacher_step(
        table, weights, (before, after), ((1, 0), (2, 0)), cols, (partial,)
    )
    far = (lax.ppermute(lower, AXES, plus), lax.ppermute(upper, AXES, minus))

    got_other = sibling(got)
    meta_all = got[:, half + cols]
    ids = (meta_all[:, 0:32].astype(jnp.int32) * 256 + meta_all[:, 32:64].astype(jnp.int32)).reshape(256)
    maskf = meta_all[:, 64:96].astype(jnp.float32).reshape(256)
    ids_half = lax.dynamic_slice_in_dim(ids, core * half, half)
    mask_half = lax.dynamic_slice_in_dim(maskf, core * half, half)

    categories = jnp.arange(temps.shape[0], dtype=jnp.int32)
    taus = jnp.sum(
        jnp.where(variant_ids[:, None] == categories[None, :], temps[None, :], 0.0), axis=1
    )
    inv_tau = jnp.repeat(1.0 / taus, half)[None]

    base = jnp.stack([(b * 8 + a) * cols, ((b + 1 - 2 * core) * 8 + a) * cols])
    l_own, l_other, s_stats = student_logits(got, got_other, ids_half[None], base, cols)
    logits = (l_own, l_other)
    e, local_top, packed = teacher_step(
        table, weights, far, ((3, 0), (3, 2)), cols, (partial,), (inv_tau, l_own, l_other, s_stats)
    )
    groups = [
        sorted(device_index(i // 16, i // 4, i, c) for i in range(64)) for c in range(2)
    ]
    gathered = lax.all_to_all(packed, AXES, 0, 0, tiled=True, axis_index_groups=groups)
    errors, loss_half = finish(
        gathered, e, logits, local_top, mask_half[None], ids_half[None],
        jnp.concatenate([base, core[None]]),
    )
    loss_half = loss_half[0]
    loss_all = ordered(core, loss_half, sibling(loss_half), 0)
    token_loss = lax.dynamic_slice_in_dim(loss_all, a * 32, 32)
    pairs = [[v * 16 + 2 * k + c for v in range(8) for c in range(2)] for k in range(8)]
    errors = lax.all_to_all(errors, AXES, 0, 0, tiled=True, axis_index_groups=pairs)
    return token_loss, student_gradient(errors, student_hidden).T


def solution(mesh):
    in_specs = (
        P(None, None, ("variant", "vocab")),
        P(None, ("vocab", "variant")),
        P(),
        P(),
        P(None, "variant"),
        P("variant", "vocab"),
        P("variant"),
        P("variant"),
    )
    out_specs = (P("variant"), P("variant", "vocab"))
    return jax.shard_map(
        on_device, mesh=mesh, in_specs=in_specs, out_specs=out_specs, check_vma=False
    )
```

```python
import functools
import math
import jax
import jax.numpy as jnp
from jax import lax
from jax.experimental import pallas as pl
from jax.experimental.pallas import tpu as pltpu
from jax.sharding import PartitionSpec as P

mix_weight = 0.5
loss_scale = 4096.0

AXES = ("variant", "vocab")
SIDE = 4
ROWS = 640
OFFSETS = (0, -1, 1, 2)


def device_index(x, y, z, c):
    x, y, z = x % SIDE, y % SIDE, z % SIDE
    return ((z % 2) * SIDE + x) * 16 + y * 4 + (z // 2) * 2 + c


def permutation(move):
    return [
        (device_index(x, y, z, c), device_index(*move(x, y, z, c)))
        for x in range(SIDE)
        for y in range(SIDE)
        for z in range(SIDE)
        for c in range(2)
    ]


def ring_shift(axes, step):
    def move(x, y, z, c):
        at = {"x": x, "y": y, "z": z}
        at[axes[c]] += step
        return at["x"], at["y"], at["z"], c

    return permutation(move)


def sibling(value):
    return lax.ppermute(value, AXES, permutation(lambda x, y, z, c: (x, y, z, 1 - c)))


def ring_gather(value, axes):
    return [value] + [
        lax.ppermute(value, AXES, ring_shift(axes, step)) for step in (1, -1, 2)
    ]


def stack_kernel(*refs):
    for i in range(4):
        if len(refs[i].shape) == 2:
            refs[-1][i] = refs[i][...]
        else:
            for j in range(4):
                refs[-1][4 * j + i] = refs[i][j]


def stack(blocks, after=()):
    vmem = pl.BlockSpec(memory_space=pltpu.VMEM)
    old = blocks[0].shape
    shape = (4,) + old if len(old) == 2 else (4 * old[0],) + old[1:]
    return pl.pallas_call(
        stack_kernel,
        out_shape=jax.ShapeDtypeStruct(shape, jnp.bfloat16),
        in_specs=[vmem] * 4 + [pl.BlockSpec(memory_space=pl.ANY)] * len(after),
        out_specs=vmem,
        cost_estimate=pl.CostEstimate(
            flops=0, bytes_accessed=4 * math.prod(shape), transcendentals=0
        ),
    )(*blocks, *after)


def halves_kernel(before, after, through_in, other, before_half, after_half, through_out):
    before_half[...] = before[...]
    after_half[...] = after[...]


def forward_halves(before, after, through, other):
    n, rows, lanes = before.shape
    block = (n // 2, rows, lanes)
    hbm = pl.BlockSpec(memory_space=pl.ANY)
    lower = pl.BlockSpec(block, lambda i: (0, 0, 0))
    return pl.pallas_call(
        halves_kernel,
        grid=(1,),
        out_shape=[jax.ShapeDtypeStruct(block, before.dtype)] * 2
        + [jax.ShapeDtypeStruct(through.shape, through.dtype)],
        in_specs=[lower, pl.BlockSpec(block, lambda i: (1, 0, 0)), hbm, hbm],
        out_specs=[lower, lower, hbm],
        input_output_aliases={2: 2},
        cost_estimate=pl.CostEstimate(
            flops=0, bytes_accessed=4 * n * rows * lanes, transcendentals=0
        ),
    )(before, after, through, other)


def reorder_kernel(w_ref, after, *out_refs):
    step = pl.program_id(0)
    cols = w_ref.shape[0]
    pairs = [w_ref[:, y * 128 : (y + 1) * 128] for y in range(SIDE)]
    for zh in range(2):
        for i in range(2):
            lane = pl.multiple_of(zh * 2048 + step * 256 + i * 128, 128)
            piece = jnp.concatenate(
                [pair[:, zh * 64 : (zh + 1) * 64] for pair in pairs[2 * i : 2 * i + 2]], axis=1
            )
            for k, out_ref in enumerate(out_refs):
                here = piece[128 * k : min(128 * (k + 1), cols)]
                out_ref[: here.shape[0], pl.ds(lane, 128)] = here


def reorder(weight, after):
    cols, width = weight.shape
    return pl.pallas_call(
        reorder_kernel,
        grid=(8,),
        out_shape=[jax.ShapeDtypeStruct((128, width), weight.dtype)] * 4,
        in_specs=[
            pl.BlockSpec((cols, 512), lambda i: (0, i)),
            pl.BlockSpec(memory_space=pl.ANY),
        ],
        out_specs=[pl.BlockSpec((128, width), lambda i: (0, 0))] * 4,
        cost_estimate=pl.CostEstimate(
            flops=0, bytes_accessed=4 * cols * width, transcendentals=0
        ),
    )(weight, after)


def finish_kernel(g_ref, e_ref, l_own, l_other, top_ref, mask_ref, ids_ref, base_ref, *outs):
    err_ref, loss_ref = outs
    cols, half = l_own.shape
    near = g_ref[:, 0:8, :]
    top = jnp.max(near, axis=0)
    lse = top + jnp.log(jnp.sum(jnp.exp(near - top), axis=0))
    soft = jnp.sum(
        jnp.sum(jnp.exp(near - lse) * g_ref[:, 8:16, :], axis=0), axis=0, keepdims=True
    ) / 8
    students = g_ref[:, 16, :]
    s_top = jnp.max(students, axis=0, keepdims=True)
    s_lse = s_top + jnp.log(jnp.sum(jnp.exp(students - s_top), axis=0, keepdims=True))
    hard = jnp.sum(g_ref[:, 17, :], axis=0, keepdims=True) - s_lse
    mask = mask_ref[...]
    loss_ref[...] = mask * (-mix_weight * (soft - s_lse) - (1.0 - mix_weight) * hard)
    factors = jnp.exp(top_ref[...] - lse) * (mix_weight / 8)
    scale = loss_scale * mask
    rows = lax.broadcasted_iota(jnp.int32, (cols, half), 0)
    core = base_ref[2]
    for i, l in enumerate((l_own, l_other)):
        value = jnp.exp(l[...] - s_lse)
        hit = rows + base_ref[i] == ids_ref[...]
        value -= jnp.where(hit, 1.0 - mix_weight, 0.0)
        averaged = e_ref[i, :, 0:half] * factors[0:1]
        for v in range(1, 8):
            averaged += e_ref[i, :, v * half : (v + 1) * half] * factors[v : v + 1]
        error = (scale * (value - averaged)).astype(jnp.bfloat16)
        target = core if i == 0 else 1 - core

        def spread(k, _, error=error, target=target):
            err_ref[2 * k + target] = error
            return 0

        lax.fori_loop(0, 8, spread, 0)


def finish(gathered, e, logits, top, mask, ids, base):
    cols, half = logits[0].shape
    vmem = pl.BlockSpec(memory_space=pltpu.VMEM)
    return pl.pallas_call(
        finish_kernel,
        out_shape=[
            jax.ShapeDtypeStruct((16, cols, half), jnp.bfloat16),
            jax.ShapeDtypeStruct((1, half), jnp.float32),
        ],
        in_specs=[vmem] * 7 + [pl.BlockSpec(memory_space=pltpu.SMEM)],
        out_specs=[vmem] * 2,
        compiler_params=pltpu.CompilerParams(vmem_limit_bytes=16 << 20),
        cost_estimate=pl.CostEstimate(
            flops=40 * cols * half, bytes_accessed=12 * cols * 1024, transcendentals=2 * cols * half
        ),
    )(gathered, e, *logits, top, mask, ids, base)


def grad_kernel(err_ref, hidden_ref, out_ref, rows_ref, sem):
    blocks, cols = err_ref.shape[0] // 2, err_ref.shape[1]
    copies, done = [], 0
    for k in range(blocks):
        error = jnp.concatenate([err_ref[2 * k], err_ref[2 * k + 1]], axis=1)
        rows_ref[k * cols : (k + 1) * cols, :] = jnp.dot(
            error, hidden_ref[...], preferred_element_type=jnp.float32
        )
        ready = (k + 1) * cols // 8 * 8
        here = pl.ds(done, ready - done)
        copies.append(pltpu.make_async_copy(rows_ref.at[here], out_ref.at[here], sem.at[k]))
        copies[-1].start()
        done = ready
    for copy in copies:
        copy.wait()


def student_gradient(errors, hidden):
    blocks, cols = errors.shape[0] // 2, errors.shape[1]
    vmem = pl.BlockSpec(memory_space=pltpu.VMEM)
    width = hidden.shape[1]
    return pl.pallas_call(
        grad_kernel,
        out_shape=jax.ShapeDtypeStruct((blocks * cols, width), jnp.float32),
        in_specs=[vmem, vmem],
        out_specs=pl.BlockSpec(memory_space=pltpu.HBM),
        scratch_shapes=[
            pltpu.VMEM((blocks * cols, width), jnp.float32),
            pltpu.SemaphoreType.DMA((blocks,)),
        ],
        compiler_params=pltpu.CompilerParams(vmem_limit_bytes=16 << 20),
        cost_estimate=pl.CostEstimate(
            flops=2 * blocks * cols * 256 * width, bytes_accessed=7 << 20, transcendentals=0
        ),
    )(errors, hidden)


def send_kernel(mine_ref, weight_ref, meta_ref, out_ref):
    blocks, half = out_ref.shape[0], mine_ref.shape[0]
    cols = weight_ref.shape[0] // blocks
    for k in range(blocks):
        out_ref[k, :half, :] = mine_ref[...]
        out_ref[k, half : half + cols, :] = weight_ref[k * cols : (k + 1) * cols, :]
        out_ref[k, half + cols :, :] = jnp.broadcast_to(
            meta_ref[...], (ROWS - half - cols, meta_ref.shape[1])
        )


def send_blocks(mine, weight, meta):
    vmem = pl.BlockSpec(memory_space=pltpu.VMEM)
    return pl.pallas_call(
        send_kernel,
        out_shape=jax.ShapeDtypeStruct((8, ROWS, mine.shape[1]), mine.dtype),
        in_specs=[vmem] * 3,
        out_specs=vmem,
        compiler_params=pltpu.CompilerParams(vmem_limit_bytes=16 << 20),
        cost_estimate=pl.CostEstimate(flops=0, bytes_accessed=9 << 20, transcendentals=0),
    )(mine, weight, meta)


def student_kernel(own_ref, other_ref, ids_ref, base_ref, l_own, l_other, stat_ref):
    half, cols = l_own.shape[1], l_own.shape[0]
    dims = (((1,), (1,)), ((), ()))
    logits = []
    for ref, out in ((own_ref, l_own), (other_ref, l_other)):
        total = jnp.zeros((cols, half), jnp.float32)
        for block in range(8):
            total += lax.dot_general(
                ref[block, half : half + cols, :],
                own_ref[block, :half, :],
                dims,
                preferred_element_type=jnp.float32,
            )
        out[...] = total
        logits.append(total)
    top = jnp.maximum(
        jnp.max(logits[0], axis=0, keepdims=True), jnp.max(logits[1], axis=0, keepdims=True)
    )
    total = jnp.zeros((1, half), jnp.float32)
    hard = jnp.zeros((1, half), jnp.float32)
    rows = lax.broadcasted_iota(jnp.int32, (cols, half), 0)
    for i in range(2):
        total += jnp.sum(jnp.exp(logits[i] - top), axis=0, keepdims=True)
        hit = rows + base_ref[i] == ids_ref[...]
        hard += jnp.sum(jnp.where(hit, logits[i], 0.0), axis=0, keepdims=True)
    stat_ref[...] = jnp.concatenate([top + jnp.log(total), hard, jnp.zeros((6, half), jnp.float32)])


def student_logits(own, other, ids, base, cols):
    half = ids.shape[1]
    vmem = pl.BlockSpec(memory_space=pltpu.VMEM)
    return pl.pallas_call(
        student_kernel,
        out_shape=[
            jax.ShapeDtypeStruct((cols, half), jnp.float32),
            jax.ShapeDtypeStruct((cols, half), jnp.float32),
            jax.ShapeDtypeStruct((8, half), jnp.float32),
        ],
        in_specs=[vmem] * 3 + [pl.BlockSpec(memory_space=pltpu.SMEM)],
        out_specs=[vmem] * 3,
        compiler_params=pltpu.CompilerParams(vmem_limit_bytes=24 << 20),
        cost_estimate=pl.CostEstimate(
            flops=2 * 2 * cols * half * 2048, bytes_accessed=12 << 20, transcendentals=2 * cols * half
        ),
    )(own, other, ids, base)


def ordered(core, own, other, axis):
    return jnp.where(
        core == 0,
        jnp.concatenate([own, other], axis=axis),
        jnp.concatenate([other, own], axis=axis),
    )


def gather_blocks(table, sources, w_refs, hidden, weights, sems):
    copies = []
    run = 0
    for ref, slot, first in sources:
        for s1 in range(first, first + ref.shape[0] // 4):
            at = run * 256
            for s2 in range(4):
                row = pl.multiple_of(at + table[16 + s2] * 64, 64)
                copies.append(
                    pltpu.make_async_copy(
                        ref.at[4 * (s1 - first) + s2], hidden.at[pl.ds(row, 64)], sems.at[0]
                    )
                )
            lane = pl.multiple_of(table[slot * 4 + s1] * 256, 256)
            for k, w in enumerate(w_refs):
                copies.append(
                    pltpu.make_async_copy(
                        w.at[:, pl.ds(lane, 256)],
                        weights.at[pl.ds(128 * k, 128), pl.ds(at, 256)],
                        sems.at[1],
                    )
                )
            run += 1
    for copy in copies:
        copy.start()
    for copy in copies:
        copy.wait()


def partial_kernel(sources, first, *refs):
    n = len(sources)
    table, w_refs, hidden_refs, refs = refs[0], refs[1:9], refs[9 : 9 + n], refs[9 + n :]
    old = None if first else refs[0]
    hidden, weights, sems = refs[-3:]
    out, done = refs[0 if first else 1], refs[1 if first else 2]
    gather_blocks(
        table, [(r,) + s for r, s in zip(hidden_refs, sources)], w_refs, hidden, weights, sems
    )
    done[...] = jnp.zeros_like(done)

    def tile(j, _):
        lanes = pl.ds(pl.multiple_of(j * 256, 256), 256)
        part = jnp.dot(weights[...], hidden[:, lanes], preferred_element_type=jnp.float32)
        out[:, lanes] = part if first else old[:, lanes] + part
        return 0

    lax.fori_loop(0, 4, tile, 0)


def last_kernel(sources, *refs):
    n = len(sources)
    table, inv_tau, w_refs = refs[0], refs[1], refs[2:10]
    hidden_refs, refs = refs[10 : 10 + n], refs[10 + n :]
    old, l_refs, student = refs[0], refs[1:3], refs[3]
    e_ref, top_ref, stat_ref = refs[4:7]
    hidden, weights, sems = refs[7:]
    cols = e_ref.shape[1]
    gather_blocks(
        table, [(r,) + s for r, s in zip(hidden_refs, sources)], w_refs, hidden, weights, sems
    )
    for j in range(4):
        lanes = slice(j * 256, j * 256 + 256)
        scale = inv_tau[:, lanes]
        part = jnp.dot(weights[...], hidden[:, lanes], preferred_element_type=jnp.float32)
        scores = [
            (old[i * 512 : i * 512 + cols, lanes] + part[i * 512 : i * 512 + cols]) * scale
            for i in range(2)
        ]
        top = jnp.maximum(
            jnp.max(scores[0], axis=0, keepdims=True), jnp.max(scores[1], axis=0, keepdims=True)
        )
        total = jnp.zeros((1, 256), jnp.float32)
        cross = jnp.zeros((1, 256), jnp.float32)
        for i in range(2):
            e = jnp.exp(scores[i] - top)
            e_ref[i, :, lanes] = e
            logits = l_refs[i][...]
            total += jnp.sum(e, axis=0, keepdims=True)
            cross += jnp.sum(
                e * jnp.concatenate([logits, logits], axis=1), axis=0, keepdims=True
            )
        lse, mean = top + jnp.log(total), cross / total
        for k in range(2):
            part, v = slice(k * 128, k * 128 + 128), 2 * j + k
            top_ref[v : v + 1, :] = top[:, part]
            stat_ref[0, v : v + 1, :] = lse[:, part]
            stat_ref[0, 8 + v : 9 + v, :] = mean[:, part]
    stat_ref[0, 16:24, :] = student[...]
    rows = stat_ref[0]

    def spread(k, _):
        stat_ref[k] = rows
        return 0

    lax.fori_loop(1, stat_ref.shape[0], spread, 0)


def teacher_step(table, weights, hidden, sources, cols, old=(), last=()):
    width = weights[0].shape[1]
    runs = sum(h.shape[0] for h in hidden) // 4
    smem = pl.BlockSpec(memory_space=pltpu.SMEM)
    vmem = pl.BlockSpec(memory_space=pltpu.VMEM)
    hbm = pl.BlockSpec(memory_space=pltpu.HBM)
    if last:
        inv_tau, *student = last
        body = functools.partial(last_kernel, sources)
        out_shape = [
            jax.ShapeDtypeStruct((2, cols, 1024), jnp.float32),
            jax.ShapeDtypeStruct((8, 128), jnp.float32),
            jax.ShapeDtypeStruct((64, 24, 128), jnp.float32),
        ]
        args = (table, inv_tau, *weights, *hidden, *old, *student)
        in_specs = [smem, vmem] + [hbm] * (8 + len(hidden)) + [vmem] * 4
        out_specs = [vmem] * 3
    else:
        body = functools.partial(partial_kernel, sources, not old)
        out_shape = [
            jax.ShapeDtypeStruct((1024, 1024), jnp.float32),
            jax.ShapeDtypeStruct((8, 128), jnp.float32),
        ]
        args = (table, *weights, *hidden, *old)
        in_specs = [smem] + [hbm] * (8 + len(hidden)) + [vmem] * len(old)
        out_specs = [vmem] * 2
    return pl.pallas_call(
        body,
        out_shape=out_shape,
        in_specs=in_specs,
        out_specs=out_specs,
        scratch_shapes=[
            pltpu.VMEM((runs * 256, 1024), jnp.bfloat16),
            pltpu.VMEM((1024, runs * 256), jnp.bfloat16),
            pltpu.SemaphoreType.DMA((2,)),
        ],
        compiler_params=pltpu.CompilerParams(vmem_limit_bytes=(52 if last else 56) << 20),
        cost_estimate=pl.CostEstimate(
            flops=2 * 1024 * runs * 256 * 1024 if last else 100 << 20,
            bytes_accessed=8 << 20 if last else 100 << 10,
            transcendentals=2 * cols * 1024 if last else 0,
        ),
    )(*args)


def on_device(
    teacher_hidden,
    teacher_weight,
    variant_ids,
    temps,
    student_hidden,
    student_weight,
    token_ids,
    loss_mask,
):
    a = lax.axis_index("variant")
    b = lax.axis_index("vocab")
    core = b % 2
    x, y, z = a % 4, b // 4, (b // 2) % 2 * 2 + a // 4
    cols = teacher_weight.shape[1]
    half = 128

    halves = [
        lax.dynamic_slice_in_dim(teacher_hidden, start * half, half, axis=1)
        .transpose(2, 0, 1)
        .reshape(32, 1024)
        for start in (core, 1 - core)
    ]
    unit = ordered(core, halves[0], sibling(halves[1]), 0)
    blocks = ring_gather(unit, "zx")

    meta = jnp.concatenate(
        [token_ids // 256, token_ids % 256, loss_mask, jnp.zeros((32,), jnp.int32)]
    ).astype(jnp.bfloat16)
    meta = jnp.concatenate([meta, unit[0, :128]])[None]
    mine = lax.dynamic_slice_in_dim(student_hidden, core * half, half, axis=0)
    send = send_blocks(mine, student_weight.T, meta)
    got = lax.all_to_all(send, "variant", 0, 0, tiled=True)

    hidden = stack(blocks, (send,))
    hidden = stack(ring_gather(hidden, "yy"))
    w_own = reorder(teacher_weight.T, unit)
    weights = (*w_own, *(sibling(w) for w in w_own))
    plus, minus = ring_shift("xz", 1), ring_shift("xz", -1)
    before = lax.ppermute(hidden, AXES, plus)
    after = lax.ppermute(hidden, AXES, minus)
    offsets = jnp.array(OFFSETS, jnp.int32)
    o1, o3 = offsets[None, :], offsets[:, None]
    px = (x + jnp.where(core == 0, o3, o1)) % 4
    pz = (z + jnp.where(core == 0, o1, o3)) % 4
    table = jnp.concatenate(
        [((pz // 2 * 2 + pz % 2) * 4 + px).reshape(16), (y + offsets) % 4]
    )
    partial, done = teacher_step(table, weights, (hidden,), ((0, 0),), cols)
    lower, upper, got = forward_halves(before, after, got, done)
    partial, done = teacher_step(
        table, weights, (before, after), ((1, 0), (2, 0)), cols, (partial,)
    )
    far = (lax.ppermute(lower, AXES, plus), lax.ppermute(upper, AXES, minus))

    got_other = sibling(got)
    meta_all = got[:, half + cols]
    ids = (meta_all[:, 0:32].astype(jnp.int32) * 256 + meta_all[:, 32:64].astype(jnp.int32)).reshape(256)
    maskf = meta_all[:, 64:96].astype(jnp.float32).reshape(256)
    ids_half = lax.dynamic_slice_in_dim(ids, core * half, half)
    mask_half = lax.dynamic_slice_in_dim(maskf, core * half, half)

    categories = jnp.arange(temps.shape[0], dtype=jnp.int32)
    taus = jnp.sum(
        jnp.where(variant_ids[:, None] == categories[None, :], temps[None, :], 0.0), axis=1
    )
    inv_tau = jnp.repeat(1.0 / taus, half)[None]

    base = jnp.stack([(b * 8 + a) * cols, ((b + 1 - 2 * core) * 8 + a) * cols])
    l_own, l_other, s_stats = student_logits(got, got_other, ids_half[None], base, cols)
    logits = (l_own, l_other)
    e, local_top, packed = teacher_step(
        table, weights, far, ((3, 0), (3, 2)), cols, (partial,), (inv_tau, l_own, l_other, s_stats)
    )
    groups = [
        sorted(device_index(i // 16, i // 4, i, c) for i in range(64)) for c in range(2)
    ]
    gathered = lax.all_to_all(packed, AXES, 0, 0, tiled=True, axis_index_groups=groups)
    errors, loss_half = finish(
        gathered, e, logits, local_top, mask_half[None], ids_half[None],
        jnp.concatenate([base, core[None]]),
    )
    loss_half = loss_half[0]
    loss_all = ordered(core, loss_half, sibling(loss_half), 0)
    token_loss = lax.dynamic_slice_in_dim(loss_all, a * 32, 32)
    pairs = [[v * 16 + 2 * k + c for v in range(8) for c in range(2)] for k in range(8)]
    errors = lax.all_to_all(errors, AXES, 0, 0, tiled=True, axis_index_groups=pairs)
    return token_loss, student_gradient(errors, student_hidden).T


def solution(mesh):
    in_specs = (
        P(None, None, ("variant", "vocab")),
        P(None, ("vocab", "variant")),
        P(),
        P(),
        P(None, "variant"),
        P("variant", "vocab"),
        P("variant"),
        P("variant"),
    )
    out_specs = (P("variant"), P("variant", "vocab"))
    return jax.shard_map(
        on_device, mesh=mesh, in_specs=in_specs, out_specs=out_specs, check_vma=False
    )
```

```python
import functools
import math
import jax
import jax.numpy as jnp
from jax import lax
from jax.experimental import pallas as pl
from jax.experimental.pallas import tpu as pltpu
from jax.sharding import PartitionSpec as P

mix_weight = 0.5
loss_scale = 4096.0

AXES = ("variant", "vocab")
SIDE = 4
ROWS = 632
OFFSETS = (0, -1, 1, 2)


def device_index(x, y, z, c):
    x, y, z = x % SIDE, y % SIDE, z % SIDE
    return ((z % 2) * SIDE + x) * 16 + y * 4 + (z // 2) * 2 + c


def permutation(move):
    return [
        (device_index(x, y, z, c), device_index(*move(x, y, z, c)))
        for x in range(SIDE)
        for y in range(SIDE)
        for z in range(SIDE)
        for c in range(2)
    ]


def ring_shift(axes, step):
    def move(x, y, z, c):
        at = {"x": x, "y": y, "z": z}
        at[axes[c]] += step
        return at["x"], at["y"], at["z"], c

    return permutation(move)


def sibling(value):
    return lax.ppermute(value, AXES, permutation(lambda x, y, z, c: (x, y, z, 1 - c)))


def ring_gather(value, axes):
    return [value] + [
        lax.ppermute(value, AXES, ring_shift(axes, step)) for step in (1, -1, 2)
    ]


def stack_kernel(*refs):
    for i in range(4):
        if len(refs[i].shape) == 2:
            refs[-1][i] = refs[i][...]
        else:
            for j in range(4):
                refs[-1][4 * j + i] = refs[i][j]


def stack(blocks, after=()):
    vmem = pl.BlockSpec(memory_space=pltpu.VMEM)
    old = blocks[0].shape
    shape = (4,) + old if len(old) == 2 else (4 * old[0],) + old[1:]
    return pl.pallas_call(
        stack_kernel,
        out_shape=jax.ShapeDtypeStruct(shape, jnp.bfloat16),
        in_specs=[vmem] * 4 + [pl.BlockSpec(memory_space=pl.ANY)] * len(after),
        out_specs=vmem,
        cost_estimate=pl.CostEstimate(
            flops=0, bytes_accessed=4 * math.prod(shape), transcendentals=0
        ),
    )(*blocks, *after)


def halves_kernel(before, after, through_in, other, before_half, after_half, through_out):
    before_half[...] = before[...]
    after_half[...] = after[...]


def forward_halves(before, after, through, other):
    n, rows, lanes = before.shape
    block = (n // 2, rows, lanes)
    hbm = pl.BlockSpec(memory_space=pl.ANY)
    lower = pl.BlockSpec(block, lambda i: (0, 0, 0))
    return pl.pallas_call(
        halves_kernel,
        grid=(1,),
        out_shape=[jax.ShapeDtypeStruct(block, before.dtype)] * 2
        + [jax.ShapeDtypeStruct(through.shape, through.dtype)],
        in_specs=[lower, pl.BlockSpec(block, lambda i: (1, 0, 0)), hbm, hbm],
        out_specs=[lower, lower, hbm],
        input_output_aliases={2: 2},
        cost_estimate=pl.CostEstimate(
            flops=0, bytes_accessed=4 * n * rows * lanes, transcendentals=0
        ),
    )(before, after, through, other)


def reorder_kernel(w_ref, after, *out_refs):
    step = pl.program_id(0)
    cols = w_ref.shape[0]
    pairs = [w_ref[:, y * 128 : (y + 1) * 128] for y in range(SIDE)]
    for zh in range(2):
        for i in range(2):
            lane = pl.multiple_of(zh * 2048 + step * 256 + i * 128, 128)
            piece = jnp.concatenate(
                [pair[:, zh * 64 : (zh + 1) * 64] for pair in pairs[2 * i : 2 * i + 2]], axis=1
            )
            for k, out_ref in enumerate(out_refs):
                here = piece[128 * k : min(128 * (k + 1), cols)]
                out_ref[: here.shape[0], pl.ds(lane, 128)] = here


def reorder(weight, after):
    cols, width = weight.shape
    return pl.pallas_call(
        reorder_kernel,
        grid=(8,),
        out_shape=[jax.ShapeDtypeStruct((128, width), weight.dtype)] * 4,
        in_specs=[
            pl.BlockSpec((cols, 512), lambda i: (0, i)),
            pl.BlockSpec(memory_space=pl.ANY),
        ],
        out_specs=[pl.BlockSpec((128, width), lambda i: (0, 0))] * 4,
        cost_estimate=pl.CostEstimate(
            flops=0, bytes_accessed=4 * cols * width, transcendentals=0
        ),
    )(weight, after)


def finish_kernel(g_ref, e_ref, l_own, l_other, top_ref, mask_ref, ids_ref, base_ref, *outs):
    err_ref, loss_ref = outs
    cols, half = l_own.shape
    near = g_ref[:, 0:8, :]
    top = jnp.max(near, axis=0)
    lse = top + jnp.log(jnp.sum(jnp.exp(near - top), axis=0))
    soft = jnp.sum(
        jnp.sum(jnp.exp(near - lse) * g_ref[:, 8:16, :], axis=0), axis=0, keepdims=True
    ) / 8
    students = g_ref[:, 16, :]
    s_top = jnp.max(students, axis=0, keepdims=True)
    s_lse = s_top + jnp.log(jnp.sum(jnp.exp(students - s_top), axis=0, keepdims=True))
    hard = jnp.sum(g_ref[:, 17, :], axis=0, keepdims=True) - s_lse
    mask = mask_ref[...]
    loss_ref[...] = mask * (-mix_weight * (soft - s_lse) - (1.0 - mix_weight) * hard)
    factors = jnp.exp(top_ref[...] - lse) * (mix_weight / 8)
    scale = loss_scale * mask
    rows = lax.broadcasted_iota(jnp.int32, (cols, half), 0)
    core = base_ref[2]
    for i, l in enumerate((l_own, l_other)):
        value = jnp.exp(l[...] - s_lse)
        hit = rows + base_ref[i] == ids_ref[...]
        value -= jnp.where(hit, 1.0 - mix_weight, 0.0)
        averaged = e_ref[i, :, 0:half] * factors[0:1]
        for v in range(1, 8):
            averaged += e_ref[i, :, v * half : (v + 1) * half] * factors[v : v + 1]
        error = (scale * (value - averaged)).astype(jnp.bfloat16)
        target = core if i == 0 else 1 - core

        def spread(k, _, error=error, target=target):
            err_ref[2 * k + target] = error
            return 0

        lax.fori_loop(0, 8, spread, 0)


def finish(gathered, e, logits, top, mask, ids, base):
    cols, half = logits[0].shape
    vmem = pl.BlockSpec(memory_space=pltpu.VMEM)
    return pl.pallas_call(
        finish_kernel,
        out_shape=[
            jax.ShapeDtypeStruct((16, cols, half), jnp.bfloat16),
            jax.ShapeDtypeStruct((1, half), jnp.float32),
        ],
        in_specs=[vmem] * 7 + [pl.BlockSpec(memory_space=pltpu.SMEM)],
        out_specs=[vmem] * 2,
        compiler_params=pltpu.CompilerParams(vmem_limit_bytes=16 << 20),
        cost_estimate=pl.CostEstimate(
            flops=40 * cols * half, bytes_accessed=12 * cols * 1024, transcendentals=2 * cols * half
        ),
    )(gathered, e, *logits, top, mask, ids, base)


def grad_kernel(err_ref, hidden_ref, out_ref, rows_ref, sem):
    blocks, cols = err_ref.shape[0] // 2, err_ref.shape[1]
    copies, done = [], 0
    for k in range(blocks):
        error = jnp.concatenate([err_ref[2 * k], err_ref[2 * k + 1]], axis=1)
        rows_ref[k * cols : (k + 1) * cols, :] = jnp.dot(
            error, hidden_ref[...], preferred_element_type=jnp.float32
        )
        ready = (k + 1) * cols // 8 * 8
        here = pl.ds(done, ready - done)
        copies.append(pltpu.make_async_copy(rows_ref.at[here], out_ref.at[here], sem.at[k]))
        copies[-1].start()
        done = ready
    for copy in copies:
        copy.wait()


def student_gradient(errors, hidden):
    blocks, cols = errors.shape[0] // 2, errors.shape[1]
    vmem = pl.BlockSpec(memory_space=pltpu.VMEM)
    width = hidden.shape[1]
    return pl.pallas_call(
        grad_kernel,
        out_shape=jax.ShapeDtypeStruct((blocks * cols, width), jnp.float32),
        in_specs=[vmem, vmem],
        out_specs=pl.BlockSpec(memory_space=pltpu.HBM),
        scratch_shapes=[
            pltpu.VMEM((blocks * cols, width), jnp.float32),
            pltpu.SemaphoreType.DMA((blocks,)),
        ],
        compiler_params=pltpu.CompilerParams(vmem_limit_bytes=16 << 20),
        cost_estimate=pl.CostEstimate(
            flops=2 * blocks * cols * 256 * width, bytes_accessed=7 << 20, transcendentals=0
        ),
    )(errors, hidden)


def send_kernel(mine_ref, weight_ref, meta_ref, out_ref):
    blocks, half = out_ref.shape[0], mine_ref.shape[0]
    cols = weight_ref.shape[0] // blocks
    for k in range(blocks):
        out_ref[k, :half, :] = mine_ref[...]
        out_ref[k, half : half + cols, :] = weight_ref[k * cols : (k + 1) * cols, :]
        out_ref[k, half + cols :, :] = jnp.broadcast_to(
            meta_ref[...], (ROWS - half - cols, meta_ref.shape[1])
        )


def send_blocks(mine, weight, meta):
    vmem = pl.BlockSpec(memory_space=pltpu.VMEM)
    return pl.pallas_call(
        send_kernel,
        out_shape=jax.ShapeDtypeStruct((8, ROWS, mine.shape[1]), mine.dtype),
        in_specs=[vmem] * 3,
        out_specs=vmem,
        compiler_params=pltpu.CompilerParams(vmem_limit_bytes=16 << 20),
        cost_estimate=pl.CostEstimate(flops=0, bytes_accessed=9 << 20, transcendentals=0),
    )(mine, weight, meta)


def student_kernel(own_ref, other_ref, ids_ref, base_ref, l_own, l_other, stat_ref):
    half, cols = l_own.shape[1], l_own.shape[0]
    dims = (((1,), (1,)), ((), ()))
    logits = []
    for ref, out in ((own_ref, l_own), (other_ref, l_other)):
        total = jnp.zeros((cols, half), jnp.float32)
        for block in range(8):
            total += lax.dot_general(
                ref[block, half : half + cols, :],
                own_ref[block, :half, :],
                dims,
                preferred_element_type=jnp.float32,
            )
        out[...] = total
        logits.append(total)
    top = jnp.maximum(
        jnp.max(logits[0], axis=0, keepdims=True), jnp.max(logits[1], axis=0, keepdims=True)
    )
    total = jnp.zeros((1, half), jnp.float32)
    hard = jnp.zeros((1, half), jnp.float32)
    rows = lax.broadcasted_iota(jnp.int32, (cols, half), 0)
    for i in range(2):
        total += jnp.sum(jnp.exp(logits[i] - top), axis=0, keepdims=True)
        hit = rows + base_ref[i] == ids_ref[...]
        hard += jnp.sum(jnp.where(hit, logits[i], 0.0), axis=0, keepdims=True)
    stat_ref[...] = jnp.concatenate([top + jnp.log(total), hard, jnp.zeros((6, half), jnp.float32)])


def student_logits(own, other, ids, base, cols):
    half = ids.shape[1]
    vmem = pl.BlockSpec(memory_space=pltpu.VMEM)
    return pl.pallas_call(
        student_kernel,
        out_shape=[
            jax.ShapeDtypeStruct((cols, half), jnp.float32),
            jax.ShapeDtypeStruct((cols, half), jnp.float32),
            jax.ShapeDtypeStruct((8, half), jnp.float32),
        ],
        in_specs=[vmem] * 3 + [pl.BlockSpec(memory_space=pltpu.SMEM)],
        out_specs=[vmem] * 3,
        compiler_params=pltpu.CompilerParams(vmem_limit_bytes=24 << 20),
        cost_estimate=pl.CostEstimate(
            flops=2 * 2 * cols * half * 2048, bytes_accessed=12 << 20, transcendentals=2 * cols * half
        ),
    )(own, other, ids, base)


def ordered(core, own, other, axis):
    return jnp.where(
        core == 0,
        jnp.concatenate([own, other], axis=axis),
        jnp.concatenate([other, own], axis=axis),
    )


def gather_blocks(table, sources, w_refs, hidden, weights, sems):
    copies = []
    run = 0
    for ref, slot, first in sources:
        for s1 in range(first, first + ref.shape[0] // 4):
            at = run * 256
            for s2 in range(4):
                row = pl.multiple_of(at + table[16 + s2] * 64, 64)
                copies.append(
                    pltpu.make_async_copy(
                        ref.at[4 * (s1 - first) + s2], hidden.at[pl.ds(row, 64)], sems.at[0]
                    )
                )
            lane = pl.multiple_of(table[slot * 4 + s1] * 256, 256)
            for k, w in enumerate(w_refs):
                copies.append(
                    pltpu.make_async_copy(
                        w.at[:, pl.ds(lane, 256)],
                        weights.at[pl.ds(128 * k, 128), pl.ds(at, 256)],
                        sems.at[1],
                    )
                )
            run += 1
    for copy in copies:
        copy.start()
    for copy in copies:
        copy.wait()


def partial_kernel(sources, first, *refs):
    n = len(sources)
    table, w_refs, hidden_refs, refs = refs[0], refs[1:9], refs[9 : 9 + n], refs[9 + n :]
    old = None if first else refs[0]
    hidden, weights, sems = refs[-3:]
    out, done = refs[0 if first else 1], refs[1 if first else 2]
    gather_blocks(
        table, [(r,) + s for r, s in zip(hidden_refs, sources)], w_refs, hidden, weights, sems
    )
    done[...] = jnp.zeros_like(done)

    def tile(j, _):
        lanes = pl.ds(pl.multiple_of(j * 256, 256), 256)
        part = jnp.dot(weights[...], hidden[:, lanes], preferred_element_type=jnp.float32)
        out[:, lanes] = part if first else old[:, lanes] + part
        return 0

    lax.fori_loop(0, 4, tile, 0)


def last_kernel(sources, *refs):
    n = len(sources)
    table, inv_tau, w_refs = refs[0], refs[1], refs[2:10]
    hidden_refs, refs = refs[10 : 10 + n], refs[10 + n :]
    old, l_refs, student = refs[0], refs[1:3], refs[3]
    e_ref, top_ref, stat_ref = refs[4:7]
    hidden, weights, sems = refs[7:]
    cols = e_ref.shape[1]
    gather_blocks(
        table, [(r,) + s for r, s in zip(hidden_refs, sources)], w_refs, hidden, weights, sems
    )
    for j in range(4):
        lanes = slice(j * 256, j * 256 + 256)
        scale = inv_tau[:, lanes]
        part = jnp.dot(weights[...], hidden[:, lanes], preferred_element_type=jnp.float32)
        scores = [
            (old[i * 512 : i * 512 + cols, lanes] + part[i * 512 : i * 512 + cols]) * scale
            for i in range(2)
        ]
        top = jnp.maximum(
            jnp.max(scores[0], axis=0, keepdims=True), jnp.max(scores[1], axis=0, keepdims=True)
        )
        total = jnp.zeros((1, 256), jnp.float32)
        cross = jnp.zeros((1, 256), jnp.float32)
        for i in range(2):
            e = jnp.exp(scores[i] - top)
            e_ref[i, :, lanes] = e
            logits = l_refs[i][...]
            total += jnp.sum(e, axis=0, keepdims=True)
            cross += jnp.sum(
                e * jnp.concatenate([logits, logits], axis=1), axis=0, keepdims=True
            )
        lse, mean = top + jnp.log(total), cross / total
        for k in range(2):
            part, v = slice(k * 128, k * 128 + 128), 2 * j + k
            top_ref[v : v + 1, :] = top[:, part]
            stat_ref[0, v : v + 1, :] = lse[:, part]
            stat_ref[0, 8 + v : 9 + v, :] = mean[:, part]
    stat_ref[0, 16:24, :] = student[...]
    rows = stat_ref[0]

    def spread(k, _):
        stat_ref[k] = rows
        return 0

    lax.fori_loop(1, stat_ref.shape[0], spread, 0)


def teacher_step(table, weights, hidden, sources, cols, old=(), last=()):
    width = weights[0].shape[1]
    runs = sum(h.shape[0] for h in hidden) // 4
    smem = pl.BlockSpec(memory_space=pltpu.SMEM)
    vmem = pl.BlockSpec(memory_space=pltpu.VMEM)
    hbm = pl.BlockSpec(memory_space=pltpu.HBM)
    if last:
        inv_tau, *student = last
        body = functools.partial(last_kernel, sources)
        out_shape = [
            jax.ShapeDtypeStruct((2, cols, 1024), jnp.float32),
            jax.ShapeDtypeStruct((8, 128), jnp.float32),
            jax.ShapeDtypeStruct((64, 24, 128), jnp.float32),
        ]
        args = (table, inv_tau, *weights, *hidden, *old, *student)
        in_specs = [smem, vmem] + [hbm] * (8 + len(hidden)) + [vmem] * 4
        out_specs = [vmem] * 3
    else:
        body = functools.partial(partial_kernel, sources, not old)
        out_shape = [
            jax.ShapeDtypeStruct((1024, 1024), jnp.float32),
            jax.ShapeDtypeStruct((8, 128), jnp.float32),
        ]
        args = (table, *weights, *hidden, *old)
        in_specs = [smem] + [hbm] * (8 + len(hidden)) + [vmem] * len(old)
        out_specs = [vmem] * 2
    return pl.pallas_call(
        body,
        out_shape=out_shape,
        in_specs=in_specs,
        out_specs=out_specs,
        scratch_shapes=[
            pltpu.VMEM((runs * 256, 1024), jnp.bfloat16),
            pltpu.VMEM((1024, runs * 256), jnp.bfloat16),
            pltpu.SemaphoreType.DMA((2,)),
        ],
        compiler_params=pltpu.CompilerParams(vmem_limit_bytes=(52 if last else 56) << 20),
        cost_estimate=pl.CostEstimate(
            flops=2 * 1024 * runs * 256 * 1024 if last else 100 << 20,
            bytes_accessed=8 << 20 if last else 100 << 10,
            transcendentals=2 * cols * 1024 if last else 0,
        ),
    )(*args)


def on_device(
    teacher_hidden,
    teacher_weight,
    variant_ids,
    temps,
    student_hidden,
    student_weight,
    token_ids,
    loss_mask,
):
    a = lax.axis_index("variant")
    b = lax.axis_index("vocab")
    core = b % 2
    x, y, z = a % 4, b // 4, (b // 2) % 2 * 2 + a // 4
    cols = teacher_weight.shape[1]
    half = 128

    halves = [
        lax.dynamic_slice_in_dim(teacher_hidden, start * half, half, axis=1)
        .transpose(2, 0, 1)
        .reshape(32, 1024)
        for start in (core, 1 - core)
    ]
    unit = ordered(core, halves[0], sibling(halves[1]), 0)
    blocks = ring_gather(unit, "zx")

    meta = jnp.concatenate(
        [token_ids // 256, token_ids % 256, loss_mask, jnp.zeros((32,), jnp.int32)]
    ).astype(jnp.bfloat16)
    meta = jnp.concatenate([meta, unit[0, :128]])[None]
    mine = lax.dynamic_slice_in_dim(student_hidden, core * half, half, axis=0)
    send = send_blocks(mine, student_weight.T, meta)
    got = lax.all_to_all(send, "variant", 0, 0, tiled=True)

    hidden = stack(blocks, (send,))
    hidden = stack(ring_gather(hidden, "yy"))
    w_own = reorder(teacher_weight.T, unit)
    weights = (*w_own, *(sibling(w) for w in w_own))
    plus, minus = ring_shift("xz", 1), ring_shift("xz", -1)
    before = lax.ppermute(hidden, AXES, plus)
    after = lax.ppermute(hidden, AXES, minus)
    offsets = jnp.array(OFFSETS, jnp.int32)
    o1, o3 = offsets[None, :], offsets[:, None]
    px = (x + jnp.where(core == 0, o3, o1)) % 4
    pz = (z + jnp.where(core == 0, o1, o3)) % 4
    table = jnp.concatenate(
        [((pz // 2 * 2 + pz % 2) * 4 + px).reshape(16), (y + offsets) % 4]
    )
    partial, done = teacher_step(table, weights, (hidden,), ((0, 0),), cols)
    lower, upper, got = forward_halves(before, after, got, done)
    partial, done = teacher_step(
        table, weights, (before, after), ((1, 0), (2, 0)), cols, (partial,)
    )
    far = (lax.ppermute(lower, AXES, plus), lax.ppermute(upper, AXES, minus))

    got_other = sibling(got)
    meta_all = got[:, half + cols]
    ids = (meta_all[:, 0:32].astype(jnp.int32) * 256 + meta_all[:, 32:64].astype(jnp.int32)).reshape(256)
    maskf = meta_all[:, 64:96].astype(jnp.float32).reshape(256)
    ids_half = lax.dynamic_slice_in_dim(ids, core * half, half)
    mask_half = lax.dynamic_slice_in_dim(maskf, core * half, half)

    categories = jnp.arange(temps.shape[0], dtype=jnp.int32)
    taus = jnp.sum(
        jnp.where(variant_ids[:, None] == categories[None, :], temps[None, :], 0.0), axis=1
    )
    inv_tau = jnp.repeat(1.0 / taus, half)[None]

    base = jnp.stack([(b * 8 + a) * cols, ((b + 1 - 2 * core) * 8 + a) * cols])
    l_own, l_other, s_stats = student_logits(got, got_other, ids_half[None], base, cols)
    logits = (l_own, l_other)
    e, local_top, packed = teacher_step(
        table, weights, far, ((3, 0), (3, 2)), cols, (partial,), (inv_tau, l_own, l_other, s_stats)
    )
    groups = [
        sorted(device_index(i // 16, i // 4, i, c) for i in range(64)) for c in range(2)
    ]
    gathered = lax.all_to_all(packed, AXES, 0, 0, tiled=True, axis_index_groups=groups)
    errors, loss_half = finish(
        gathered, e, logits, local_top, mask_half[None], ids_half[None],
        jnp.concatenate([base, core[None]]),
    )
    loss_half = loss_half[0]
    loss_all = ordered(core, loss_half, sibling(loss_half), 0)
    token_loss = lax.dynamic_slice_in_dim(loss_all, a * 32, 32)
    pairs = [[v * 16 + 2 * k + c for v in range(8) for c in range(2)] for k in range(8)]
    errors = lax.all_to_all(errors, AXES, 0, 0, tiled=True, axis_index_groups=pairs)
    return token_loss, student_gradient(errors, student_hidden).T


def solution(mesh):
    in_specs = (
        P(None, None, ("variant", "vocab")),
        P(None, ("vocab", "variant")),
        P(),
        P(),
        P(None, "variant"),
        P("variant", "vocab"),
        P("variant"),
        P("variant"),
    )
    out_specs = (P("variant"), P("variant", "vocab"))
    return jax.shard_map(
        on_device, mesh=mesh, in_specs=in_specs, out_specs=out_specs, check_vma=False
    )
```
